256 devices in a mesh: zonal: 64 (over y_lo, x, z), merid: 4 (over y_hi, core).
Axes of the slice: x: 4, y: 4 (y_hi: 2, y_lo: 2; y = y_hi * 2 + y_lo), z: 8, core: 2. Of those that a mesh axis runs over, the one named last changes fastest.
Arguments:
- field: bfloat16 [64, 4096, 256], P('merid', 'zonal'), may hold values from -6 to 6
- weight_one: bfloat16 [3, 3, 256, 256], replicated, may hold values from -0.125 to 0.125
- bias_one: float32 [256], replicated, may hold values from -3 to 3
- weight_two: bfloat16 [3, 3, 256, 256], replicated, may hold values from -0.125 to 0.125
- bias_two: float32 [256], replicated, may hold values from -3 to 3
- depth_levels: int32 [64, 4096], P('merid', 'zonal'), may hold values from 0 to 64
- fold_partner: int32 [4096], replicated, may hold values from 0 to 4095, as said below
- cotangent: bfloat16 [64, 4096, 256], P('merid', 'zonal'), may hold values from -6 to 6
Outputs:
- output: bfloat16 [64, 4096, 256], P('merid', 'zonal')
- input_grad: bfloat16 [64, 4096, 256], P('merid', 'zonal')
- grad_one: float32 [3, 3, 256, 256], replicated
- grad_two: float32 [3, 3, 256, 256], replicated
The draws below stay inside these ranges and needn't reach their ends.
Inputs may be any that keep to these rules, and one draw needn't show every extreme that they name: fold_partner[i] = (4095 - i + s) mod 4096 with one pivot offset s, 0 to 4095, for the whole table.
All inputs are finite; a program needn't handle non-finite values.
Results may differ from the reference program's by a relative error of at most 0.003.
Values may be sent and summed in bfloat16 or wider, within the bound.
No kernel may reach another device: no remote copies, remote signals or barrier semaphores. Data moves between devices by JAX's collectives and lax.ppermute only.
A program may use at most 128 MiB of HBM per device.

```python
import math
from functools import partial
import jax
import jax.numpy as jnp
from jax import lax

C = 256
LEV = 64
NY = 64
NX = 4096


def draw_fold_partner(key, part):
    offset = jax.random.randint(key, (), 0, NX, dtype=jnp.int32)
    index = jnp.arange(NX, dtype=jnp.int32)
    return (NX - 1 - index + offset) % NX


def touch_ends(values, own_key, smallest, largest):
    extent = values.shape
    spot = [jax.random.randint(jax.random.fold_in(own_key, axis), (), 0, extent[axis]) for axis in range(len(extent))]
    values = values.at[tuple(spot)].set(smallest)
    longest = extent.index(max(extent))
    spot[longest] = (spot[longest] + 1) % extent[longest]
    return values.at[tuple(spot)].set(largest)


def steps_of(rng, shape, split, smallest, top_value):
    loudness = 1.0
    for dim, parts in split:
        heights = jax.random.uniform(jax.random.fold_in(jax.random.fold_in(rng, 6), dim), (parts,), jnp.float32, smallest / len(split), top_value / len(split))
        loudness = loudness * jnp.repeat(jnp.exp(heights), shape[dim] // parts).reshape((-1,) + (1,) * (len(shape) - 1 - dim))
    return loudness


def bell_draw(key, extent, width, limit, pieces=(), held_as=jnp.bfloat16):
    array = width * jax.random.normal(key, extent, jnp.float32)
    if pieces:
        array = array * steps_of(key, extent, pieces, -0.22, 0.18)
    return jnp.clip(array, -limit, limit).astype(held_as)


def setup_inputs(seed: int = 0) -> dict:
    key_of = jax.random.split(jax.random.key(seed), 9)
    field = bell_draw(key_of[0], (NY, NX, C), 1.0, 6.0, ((0, 4), (1, 64)))
    weight_one = bell_draw(key_of[1], (3, 3, C, C), (9 * C) ** -0.5, 0.125)
    bias_one = bell_draw(key_of[2], (C,), 0.5, 3.0, (), jnp.float32)
    weight_two = bell_draw(key_of[3], (3, 3, C, C), (9 * C) ** -0.5, 0.125)
    bias_two = bell_draw(key_of[4], (C,), 0.5, 3.0, (), jnp.float32)
    depth_levels = touch_ends(jax.random.randint(key_of[5], (NY, NX), 0, LEV + 1), jax.random.fold_in(key_of[5], 1), 0, LEV).astype(jnp.int32)
    fold_partner = draw_fold_partner(jax.random.fold_in(key_of[8], 71), 0)
    cotangent = bell_draw(key_of[7], (NY, NX, C), 1.0, 6.0, ((0, 4), (1, 64)))
    return {"field": field, "weight_one": weight_one, "bias_one": bias_one, "weight_two": weight_two, "bias_two": bias_two, "depth_levels": depth_levels, "fold_partner": fold_partner, "cotangent": cotangent}


def pad_whole(values, fold_partner):
    fold_row = jnp.take(values[-1], fold_partner, axis=0)
    with_rows = jnp.concatenate([jnp.zeros_like(values[:1]), values, fold_row[None]], axis=0)
    return jnp.concatenate([with_rows[:, -1:], with_rows, with_rows[:, :1]], axis=1)

def convolve(padded, weight):
    result = jnp.zeros((NY, NX, weight.shape[3]), padded.dtype)
    for row_step in range(3):
        for col_step in range(3):
            window = padded[row_step:row_step + NY, col_step:col_step + NX]
            result = result + jnp.einsum('yxc,cd->yxd', window, weight[row_step, col_step], precision=lax.Precision.HIGHEST)
    return result

def reference(field, weight_one, bias_one, weight_two, bias_two, depth_levels, fold_partner, cotangent):
    level_index = jnp.arange(C, dtype=jnp.int32) % LEV
    mask = (level_index[None, None, :] < depth_levels[:, :, None]).astype(jnp.float32)
    field_pad = pad_whole(field, fold_partner).astype(jnp.float32)
    pre_one, back_one = jax.vjp(convolve, field_pad, weight_one.astype(jnp.float32))
    pre_one = pre_one + bias_one
    hidden = lax.optimization_barrier((jax.nn.gelu(pre_one) * mask).astype(jnp.bfloat16))
    hidden_pad = pad_whole(hidden, fold_partner).astype(jnp.float32)
    pre_two, back_two = jax.vjp(convolve, hidden_pad, weight_two.astype(jnp.float32))
    output = ((field.astype(jnp.float32) + pre_two + bias_two) * mask).astype(jnp.bfloat16)
    masked_grad = cotangent.astype(jnp.float32) * mask
    delta_two = lax.optimization_barrier(masked_grad.astype(jnp.bfloat16)).astype(jnp.float32)
    hidden_pad_grad, weight_two_grad = back_two(delta_two)
    _, pad_back = jax.vjp(partial(pad_whole, fold_partner=fold_partner), jnp.zeros((NY, NX, C), jnp.float32))
    hidden_grad = pad_back(hidden_pad_grad)[0]
    _, gelu_back = jax.vjp(jax.nn.gelu, pre_one)
    delta_one = gelu_back(hidden_grad * mask)[0]
    delta_one = lax.optimization_barrier(delta_one.astype(jnp.bfloat16)).astype(jnp.float32)
    field_pad_grad, weight_one_grad = back_one(delta_one)
    input_grad = (masked_grad + pad_back(field_pad_grad)[0]).astype(jnp.bfloat16)
    scale = 1.0 / math.sqrt(NY * NX)
    return (output, input_grad, weight_one_grad * scale, weight_two_grad * scale)
```

```python
import math

import jax
import jax.numpy as jnp
from jax import lax
from jax.experimental import pallas as pl
from jax.experimental.pallas import tpu as pltpu
from jax.sharding import Mesh
from jax.sharding import PartitionSpec as P

LEV = 64
SPLIT = (2, 4, 8)
ZONAL = ("yl", "x", "z")
MERID = ("yh", "c")
PLANE = ("yl", "x", "yh")
SCALE = 1.0 / 512.0
ROWS = 16
COLS = 64
CH = 256
PITCH = 72
EXT = 20 * PITCH + 16
MID = 18 * PITCH + 8
INNER = 16 * PITCH
LANES = 2 * CH + 128
HEAD = 8
F32 = jnp.float32
BF16 = jnp.bfloat16
C0 = math.sqrt(2.0 / math.pi)
C1 = 0.044715


def dot(a, b, dims=((1,), (0,))):
    return lax.dot_general(a, b, (dims, ((), ())), preferred_element_type=F32)


def taps(lhs_ref, row, count, w_ref, picks, transposed):
    total = None
    for a, b, index in picks:
        lhs = lhs_ref[row + a * PITCH : row + a * PITCH + count, b * CH : (b + 1) * CH]
        part = dot(lhs, w_ref[index], ((1,), (1 if transposed else 0,)))
        total = part if total is None else total + part
    return total


def plain(rows_of=(0, 1, 2)):
    return [(a, b, 3 * a + b) for a in rows_of for b in range(3)]


def turned(rows_of=(0, 1, 2)):
    return [(a, b, 8 - 3 * a - b) for a in rows_of for b in range(3)]


def shifted(out_ref, src_ref, count):
    step = 112
    for start in range(0, count, step):
        size = min(step, count - start)
        for b in range(3):
            at = HEAD + start + b - 1
            out_ref[start : start + size, b * CH : (b + 1) * CH] = src_ref[at : at + size, :].astype(BF16)


def own_cells(count, first):
    place = (lax.broadcasted_iota(jnp.int32, (count, CH), 0) + first) % PITCH
    return place >= 8


def transposed_own(ref, first, out_ref):
    eye = (
        lax.broadcasted_iota(jnp.int32, (CH, CH), 0) == lax.broadcasted_iota(jnp.int32, (CH, CH), 1)
    ).astype(BF16)
    step = 128
    for start in range(0, INNER, step):
        cells = ref[first + start : first + start + step, CH : 2 * CH].astype(F32)
        cells = jnp.where(own_cells(step, start), cells, 0.0).astype(BF16)
        out_ref[:, start : start + step] = dot(eye, cells, ((1,), (1,))).astype(BF16)


def weight_grad(keep_ref, send_ref, core, turned_ref, patches_ref, row):
    for a in range(3):
        for b in range(3):
            cells = patches_ref[row + a * PITCH : row + a * PITCH + INNER, b * CH : (b + 1) * CH]
            at = (3 * a + b) * CH
            sums = dot(turned_ref[...], cells)
            low, high = sums[: CH // 2], sums[CH // 2 :]
            keep_ref[:, at : at + CH] = jnp.where(core == 0, low, high)
            send_ref[:, at : at + CH] = jnp.where(core == 0, high, low)


def first_kernel(
    scal_ref, field_ref, cot_ref, dep_ref, west_ref, east_ref, south_ref, north_ref, fold_ref,
    w_ref, bias_ref,
    pf_ref, pd_ref, ph_ref, slope_ref, keep_ref, send_ref,
    ext, depth, west, east, south, north, back,
):
    top = scal_ref[0] == 1
    west[...] = west_ref[...].astype(F32)
    east[...] = east_ref[...].astype(F32)
    south[...] = south_ref[...].astype(F32)
    to = lax.broadcasted_iota(jnp.int32, (PITCH, 2 * PITCH), 0)
    at = lax.broadcasted_iota(jnp.int32, (PITCH, 2 * PITCH), 1)
    want = 63 - jnp.where(to >= 70, to - PITCH, to) + scal_ref[1]
    near = at < PITCH
    here = jnp.where(at >= 70, at - PITCH, at)
    have = jnp.where(near, jnp.where((at >= 64) & (at < 70), -99, here), at - PITCH + 64)
    have = jnp.where(at >= PITCH + 66, -99, have)
    want = jnp.where((to >= 66) & (to < 70), -98, want)
    pick = (want == have).astype(F32).astype(BF16)
    for j in range(2):
        i = 1 - j
        blocks = jnp.concatenate(
            [
                fold_ref[i * PITCH : (i + 1) * PITCH, :],
                fold_ref[(2 + i) * PITCH : (3 + i) * PITCH, :],
            ],
            axis=0,
        )
        north[j * PITCH : (j + 1) * PITCH, :] = north_ref[j * PITCH : (j + 1) * PITCH, :].astype(F32) + dot(pick, blocks)

    def fill(out_ref, lanes, own, width, head):
        if head:
            out_ref[0:head, :] = jnp.zeros((head, width), F32)
        for g in range(21):
            base = head + g * PITCH
            out_ref[base : base + 8, :] = jnp.zeros((8, width), F32)
            y = g - 3
            if 0 <= y < 16:
                out_ref[base : base + 2, :] = east[2 * y : 2 * y + 2, lanes]
            elif -2 <= y < 0:
                at = (y + 2) * PITCH + 64
                out_ref[base : base + 2, :] = south[at : at + 2, lanes]
            elif y >= 16:
                at = (y - 16) * PITCH + 64
                out_ref[base : base + 2, :] = north[at : at + 2, lanes]
            y = g - 2
            if 0 <= y < 16:
                out_ref[base + 6 : base + 8, :] = west[2 * y : 2 * y + 2, lanes]
            elif -2 <= y < 0:
                at = (y + 2) * PITCH + 70
                out_ref[base + 6 : base + 8, :] = south[at : at + 2, lanes]
            elif 16 <= y < 18:
                at = (y - 16) * PITCH + 70
                out_ref[base + 6 : base + 8, :] = north[at : at + 2, lanes]
        for y in range(-2, 18):
            base = head + (y + 2) * PITCH + 8
            if y < 0:
                out_ref[base : base + 64, :] = south[(y + 2) * PITCH : (y + 2) * PITCH + 64, lanes]
            elif y < 16:
                out_ref[base : base + 64, :] = own(y)
            else:
                out_ref[base : base + 64, :] = north[(y - 16) * PITCH : (y - 16) * PITCH + 64, lanes]
        tail = head + 20 * PITCH + 8
        rest = out_ref.shape[0] - tail
        if rest:
            out_ref[tail:, :] = jnp.zeros((rest, width), F32)

    level = lax.broadcasted_iota(jnp.int32, (1, CH), 1) % LEV
    level = level.astype(F32)

    def wet(values):
        return level < jnp.concatenate([values, values], axis=1)

    def own_field(y):
        return field_ref[y * 64 : (y + 1) * 64, :].astype(F32)

    def own_depth(y):
        return dep_ref[y * 64 : (y + 1) * 64, :].astype(F32)

    def own_delta(y):
        cells = cot_ref[y * 64 : (y + 1) * 64, :].astype(F32)
        return jnp.where(wet(own_depth(y)), cells, 0.0)

    fill(ext, slice(0, CH), own_field, CH, HEAD)
    fill(depth, slice(2 * CH, LANES), own_depth, 128, 0)
    shifted(pf_ref, ext, EXT)
    fill(ext, slice(CH, 2 * CH), own_delta, CH, HEAD)
    shifted(pd_ref, ext, EXT)

    bias = bias_ref[...]

    def finish(pre, p):
        count = pre.shape[0]
        x = pre + bias
        square = x * x
        t = jnp.tanh(C0 * (x + C1 * (square * x)))
        keep = wet(depth[p : p + count, :])
        half = 0.5 * (1.0 + t)
        hidden = jnp.where(keep, x * half, 0.0).astype(BF16).astype(F32)
        slope = half + (0.5 * C0) * x * (1.0 - t * t) * (1.0 + (3.0 * C1) * square)
        return hidden, jnp.where(keep, slope, 0.0)

    first = 72
    step = 176
    for start in range(first, first + 1232, step):
        hidden, slope = finish(taps(pf_ref, start - PITCH, step, w_ref, plain(), False), start)
        ext[HEAD + start - first : HEAD + start - first + step, :] = hidden
        slope_ref[start - first : start - first + step, :] = slope
    start = 1296
    picks = [(a, b, jnp.where(top, 8 - 3 * a - b, 3 * a + b)) for a in range(3) for b in range(3)]
    hidden, slope = finish(taps(pf_ref, start - PITCH, 80, w_ref, picks, False), start)
    at = start - first
    beyond = lax.broadcasted_iota(jnp.int32, (8, CH), 0) >= 4
    ext[HEAD + at : HEAD + at + 8, :] = jnp.where(beyond, hidden[:8], ext[HEAD + at : HEAD + at + 8, :])
    slope_ref[at : at + 8, :] = jnp.where(beyond, slope[:8], slope_ref[at : at + 8, :])
    ext[HEAD + at + 8 : HEAD + at + 80, :] = hidden[8:]
    slope_ref[at + 8 : at + 80, :] = slope[8:]
    ext[HEAD + MID : HEAD + MID + 8, :] = jnp.zeros((8, CH), F32)
    shifted(ph_ref, ext, MID)
    transposed_own(pd_ref, 144, back)
    weight_grad(keep_ref, send_ref, scal_ref[2], back, ph_ref, 0)


def second_kernel(
    scal_ref, pd_ref, pf_ref, slope_ref, w_ref, pe_ref, keep_ref, send_ref, ext, back
):
    top = scal_ref[0] == 1
    first = 72
    ext[0:HEAD, :] = jnp.zeros((HEAD, CH), F32)
    ext[HEAD + MID : HEAD + MID + 8, :] = jnp.zeros((8, CH), F32)

    def put(sums, p):
        at = p - first
        count = sums.shape[0]
        delta = (slope_ref[at : at + count, :] * sums).astype(BF16).astype(F32)
        ext[HEAD + at : HEAD + at + count, :] = delta

    step = 232
    for start in range(first, first + 1160, step):
        put(taps(pd_ref, start - PITCH, step, w_ref, turned(), True), start)
    start = 1232
    sums = taps(pd_ref, start - PITCH, 144, w_ref, turned((0,)), True)
    over = [(2, b, jnp.where(top, 6 + b, 2 - b)) for b in range(3)]
    sums = sums + taps(pd_ref, start - PITCH, 144, w_ref, over, True)
    middle = taps(pd_ref, start - PITCH, 72, w_ref, turned((1,)), True)
    beside = [(1, b, jnp.where(top, 3 + b, 5 - b)) for b in range(3)]
    upper = taps(pd_ref, 1296 - PITCH, 80, w_ref, beside, True)
    beyond = lax.broadcasted_iota(jnp.int32, (8, CH), 0) >= 4
    put(sums[:64] + middle[:64], 1232)
    put(sums[64:72] + jnp.where(beyond, upper[:8], middle[64:]), 1296)
    put(sums[72:] + upper[8:], 1304)
    start = 1224
    gap = taps(pd_ref, start - PITCH, 16, w_ref, turned((0, 1)), True)
    gap = gap + taps(pd_ref, start - PITCH, 16, w_ref, over, True)
    at = start - first
    delta = (slope_ref[at : at + 8, :] * gap[:8]).astype(BF16).astype(F32)
    ext[HEAD + at : HEAD + at + 8, :] = jnp.where(beyond, delta, ext[HEAD + at : HEAD + at + 8, :])
    shifted(pe_ref, ext, MID)
    transposed_own(pe_ref, 72, back)
    weight_grad(keep_ref, send_ref, scal_ref[2], back, pf_ref, 72)


def third_kernel(
    scal_ref, ph_ref, pe_ref, pf_ref, pd_ref, dep_ref, w1_ref, w2_ref, bias_ref, out_ref, in_ref
):
    top = scal_ref[0] == 1
    level = (lax.broadcasted_iota(jnp.int32, (1, CH), 1) % LEV).astype(F32)
    bias = bias_ref[...]
    for y in range(0, 16, 4):
        p = 144 + y * PITCH
        sums = taps(ph_ref, p - 144, 4 * PITCH, w2_ref, plain(), False)
        for k in range(4):
            at = p + k * PITCH + 8
            cells = pf_ref[at : at + 64, CH : 2 * CH].astype(F32) + sums[k * PITCH + 8 : (k + 1) * PITCH] + bias
            deep = dep_ref[(y + k) * 64 : (y + k + 1) * 64, :].astype(F32)
            keep = level < jnp.concatenate([deep, deep], axis=1)
            out_ref[(y + k) * 64 : (y + k + 1) * 64, :] = jnp.where(keep, cells, 0.0).astype(BF16)

    def put(cells, y):
        at = 144 + y * PITCH + 8
        total = pd_ref[at : at + 64, CH : 2 * CH].astype(F32) + cells
        in_ref[y * 64 : (y + 1) * 64, :] = total.astype(BF16)

    for y in range(0, 15, 5):
        p = 144 + y * PITCH
        sums = taps(pe_ref, p - 144, 5 * PITCH, w1_ref, turned(), True)
        for k in range(5):
            put(sums[k * PITCH + 8 : (k + 1) * PITCH], y + k)
    p = 144 + 15 * PITCH + 8
    over = [(2, b, jnp.where(top, 6 + b, 2 - b)) for b in range(3)]
    sums = taps(pe_ref, p - 144, 64, w1_ref, turned((0, 1)), True)
    put(sums + taps(pe_ref, p - 144, 64, w1_ref, over, True), 15)


def last_kernel(scal_ref, mine_ref, other_ref, one_ref, two_ref):
    first = scal_ref[2] == 0
    down = lax.broadcasted_iota(jnp.int32, (CH, CH), 0)
    across = lax.broadcasted_iota(jnp.int32, (CH, CH), 1)
    eye = jnp.where(down == across, SCALE, 0.0).astype(BF16)
    for k in range(18):
        mine = mine_ref[:, k * CH : (k + 1) * CH]
        other = other_ref[:, k * CH : (k + 1) * CH]
        low, high = jnp.where(first, mine, other), jnp.where(first, other, mine)
        kernel = dot(eye, jnp.concatenate([low, high], axis=0), ((1,), (1,)))
        out_ref, at = (one_ref, k) if k < 9 else (two_ref, k - 9)
        out_ref[at * CH : (at + 1) * CH, :] = kernel


VM = pl.BlockSpec(memory_space=pltpu.VMEM)
SM = pl.BlockSpec(memory_space=pltpu.SMEM)


def call(body, name, outs, scratch, *args):
    return pl.pallas_call(
        body,
        name=name,
        out_shape=[jax.ShapeDtypeStruct(s, t) for s, t in outs],
        in_specs=[SM] + [VM] * (len(args) - 1),
        out_specs=[VM] * len(outs),
        scratch_shapes=scratch,
        compiler_params=pltpu.CompilerParams(vmem_limit_bytes=60 << 20),
    )(*args)


def shards(
    field, weight_one, bias_one, weight_two, bias_two, depth_levels, fold_partner, cotangent
):
    n_low = lax.axis_size("z")
    n_high = lax.axis_size("yl") * lax.axis_size("x")
    n_z, n_m = n_low * n_high, 4
    merid = lax.axis_index(MERID)
    core = lax.axis_index("c")
    deep = jnp.broadcast_to(depth_levels[:, :, None].astype(BF16), (ROWS, COLS, 128))

    def packed(y, x):
        cut_depth = depth_levels[y, x][:, :, None]
        level = lax.broadcasted_iota(jnp.int32, (1, 1, CH), 2) % LEV
        own = jnp.where(level < cut_depth, cotangent[y, x], jnp.zeros((), BF16))
        return jnp.concatenate([field[y, x], own, deep[y, x]], axis=2)

    whole = slice(None)
    east_edge = packed(whole, slice(COLS - 2, COLS)).reshape(2 * ROWS, LANES)
    west_edge = packed(whole, slice(0, 2)).reshape(2 * ROWS, LANES)
    forward = [(i, (i + 1) % n_z) for i in range(n_z)]
    backward = [((i + 1) % n_z, i) for i in range(n_z)]
    west = lax.ppermute(east_edge, ZONAL, forward)
    east = lax.ppermute(west_edge, ZONAL, backward)

    def strip(y):
        rows = slice(y, y + 2)
        left = west[2 * y : 2 * y + 4].reshape(2, 2, LANES)
        right = east[2 * y : 2 * y + 4].reshape(2, 2, LANES)
        gap = jnp.zeros((2, 4, LANES), BF16)
        return jnp.concatenate([packed(rows, whole), right, gap, left], axis=1).reshape(2 * PITCH, LANES)

    upper, lower = strip(ROWS - 2), strip(0)
    south = lax.ppermute(upper, MERID, [(i, i + 1) for i in range(n_m - 1)])
    north = lax.ppermute(lower, MERID, [(i + 1, i) for i in range(n_m - 1)])
    shift = (fold_partner[0] + 1) % (n_z * COLS)
    quotient, rest = shift // COLS, shift % COLS

    def hop(rows, target):
        route = [(m * n_m + n_m - 1, (target(m) % n_z) * n_m + n_m - 1) for m in range(n_z)]
        return lax.ppermute(rows, ZONAL + MERID, route)

    def turn(rows, high):
        return hop(rows, lambda m: n_z - 1 + n_low * high - m)

    def slide(rows, low):
        return jnp.concatenate([hop(rows, lambda m: m + low), hop(rows, lambda m: m + low + 1)], axis=0)

    fold = lax.switch(quotient // n_low, [lambda rows, h=h: turn(rows, h) for h in range(n_high)], upper)
    fold = lax.switch(quotient % n_low, [lambda rows, h=h: slide(rows, h) for h in range(n_low)], fold)

    scal = jnp.stack([(merid == n_m - 1).astype(jnp.int32), rest.astype(jnp.int32), core.astype(jnp.int32)])
    flat_field = field.reshape(ROWS * COLS, CH)
    flat_cot = cotangent.reshape(ROWS * COLS, CH)
    flat_deep = deep.reshape(ROWS * COLS, 128)
    w1 = weight_one.reshape(9, CH, CH)
    w2 = weight_two.reshape(9, CH, CH)
    half = ((CH // 2, 9 * CH), F32)
    pf, pd, ph, slope, keep_two, send_two = call(
        first_kernel,
        "forward_block",
        [((EXT, 3 * CH), BF16), ((EXT, 3 * CH), BF16), ((MID, 3 * CH), BF16), ((MID, CH), F32), half, half],
        [
            pltpu.VMEM((EXT + 16, CH), F32),
            pltpu.VMEM((EXT, 128), F32),
            pltpu.VMEM((32, LANES), F32),
            pltpu.VMEM((32, LANES), F32),
            pltpu.VMEM((2 * PITCH, LANES), F32),
            pltpu.VMEM((2 * PITCH, LANES), F32),
            pltpu.VMEM((CH, INNER), BF16),
        ],
        scal, flat_field, flat_cot, flat_deep, west, east, south, north, fold, w1, bias_one.reshape(1, CH),
    )
    swap = [(0, 1), (1, 0)]
    came_two = lax.ppermute(send_two, "c", swap)
    pe, keep_one, send_one = call(
        second_kernel,
        "backward_block",
        [((MID, 3 * CH), BF16), half, half],
        [pltpu.VMEM((MID + 16, CH), F32), pltpu.VMEM((CH, INNER), BF16)],
        scal, pd, pf, slope, w2,
    )
    came_one = lax.ppermute(send_one, "c", swap)
    output, input_grad = call(
        third_kernel,
        "outputs_block",
        [((ROWS * COLS, CH), BF16), ((ROWS * COLS, CH), BF16)],
        [],
        scal, ph, pe, pf, pd, flat_deep, w1, w2, bias_two.reshape(1, CH),
    )

    n_p = lax.axis_size("yl") * lax.axis_size("x") * lax.axis_size("yh")
    rows = CH // 2 // n_p
    width = 18 * CH
    sums = jnp.concatenate([keep_one + came_one, keep_two + came_two], axis=1).astype(BF16)
    sums = lax.all_to_all(sums.reshape(n_p, rows, width), PLANE, 0, 0)
    sums = jnp.sum(sums.astype(F32), axis=0)
    part = rows // n_low
    sums = lax.all_to_all(sums.reshape(n_low, part * 36, 128), "z", 0, 0)
    piece = jnp.sum(sums, axis=0).astype(BF16)
    line = lax.all_to_all(jnp.broadcast_to(piece[None], (n_low, part * 36, 128)), "z", 0, 0)
    line = line.reshape(rows, width)
    mine = lax.all_to_all(jnp.broadcast_to(line[None], (n_p, rows, width)), PLANE, 0, 0)
    mine = mine.reshape(CH // 2, width)
    other = lax.ppermute(mine, "c", swap)
    grad_one, grad_two = call(
        last_kernel,
        "kernel_grads",
        [((9 * CH, CH), F32), ((9 * CH, CH), F32)],
        [],
        scal, mine, other,
    )
    return (
        output.reshape(ROWS, COLS, CH),
        input_grad.reshape(ROWS, COLS, CH),
        grad_one.reshape(3, 3, CH, CH),
        grad_two.reshape(3, 3, CH, CH),
    )


def solution(mesh):
    fine = Mesh(mesh.devices.reshape(SPLIT + (2, 2)), ZONAL + MERID)
    cells = P(MERID, ZONAL, None)
    return jax.shard_map(
        shards,
        mesh=fine,
        in_specs=(cells, P(), P(), P(), P(), P(MERID, ZONAL), P(), cells),
        out_specs=(cells, cells, P(), P()),
        check_vma=False,
    )
```

```python
import math

import jax
import jax.numpy as jnp
from jax import lax
from jax.experimental import pallas as pl
from jax.experimental.pallas import tpu as pltpu
from jax.sharding import Mesh
from jax.sharding import PartitionSpec as P


LEV = 64
SPLIT = (2, 4, 8)
ZONAL = ("yl", "x", "z")
MERID = ("yh", "c")
PLANE = ("yl", "x", "yh")
SCALE = 1.0 / 512.0
ROWS = 16
COLS = 64
CH = 256
PITCH = 72
EXT = 20 * PITCH + 16
MID = 18 * PITCH + 8
INNER = 16 * PITCH
LANES = 2 * CH + 128
HEAD = 8
F32 = jnp.float32
BF16 = jnp.bfloat16
C0 = math.sqrt(2.0 / math.pi)
C1 = 0.044715


def dot(a, b, dims=((1,), (0,))):
    return lax.dot_general(a, b, (dims, ((), ())), preferred_element_type=F32)


def taps(lhs_ref, row, count, w_ref, picks, transposed):
    total = None
    for a, indices in picks:
        lhs = lhs_ref[row + a * PITCH : row + a * PITCH + count, :]
        side = jnp.concatenate([w_ref[k] for k in indices], axis=1 if transposed else 0)
        part = dot(lhs, side, ((1,), (1 if transposed else 0,)))
        total = part if total is None else total + part
    return total


def plain(rows_of=(0, 1, 2)):
    return [(a, [3 * a + b for b in range(3)]) for a in rows_of]


def turned(rows_of=(0, 1, 2)):
    return [(a, [8 - 3 * a - b for b in range(3)]) for a in rows_of]


def shifted(out_ref, src_ref, count):
    step = 112
    for start in range(0, count, step):
        size = min(step, count - start)
        for b in range(3):
            at = HEAD + start + b - 1
            out_ref[start : start + size, b * CH : (b + 1) * CH] = src_ref[at : at + size, :].astype(BF16)


def own_cells(count, first):
    place = (lax.broadcasted_iota(jnp.int32, (count, CH), 0) + first) % PITCH
    return place >= 8


def transposed_own(ref, first, out_ref):
    eye = (
        lax.broadcasted_iota(jnp.int32, (CH, CH), 0) == lax.broadcasted_iota(jnp.int32, (CH, CH), 1)
    ).astype(BF16)
    step = 128
    for start in range(0, INNER, step):
        cells = ref[first + start : first + start + step, CH : 2 * CH].astype(F32)
        cells = jnp.where(own_cells(step, start), cells, 0.0).astype(BF16)
        out_ref[:, start : start + step] = dot(eye, cells, ((1,), (1,))).astype(BF16)


def weight_grad(keep_ref, send_ref, core, turned_ref, patches_ref, row):
    for a in range(3):
        for b in range(3):
            cells = patches_ref[row + a * PITCH : row + a * PITCH + INNER, b * CH : (b + 1) * CH]
            at = (3 * a + b) * CH
            sums = dot(turned_ref[...], cells)
            low, high = sums[: CH // 2], sums[CH // 2 :]
            keep_ref[:, at : at + CH] = jnp.where(core == 0, low, high)
            send_ref[:, at : at + CH] = jnp.where(core == 0, high, low)


def pack_kernel(field_ref, cot_ref, dep_ref, deep_ref, top_ref, low_ref, west_ref, east_ref, edge):
    eye = (
        lax.broadcasted_iota(jnp.int32, (COLS, COLS), 0) == lax.broadcasted_iota(jnp.int32, (COLS, COLS), 1)
    ).astype(F32)
    ones = jnp.ones((COLS, 128), BF16)
    level = (lax.broadcasted_iota(jnp.int32, (1, CH), 1) % LEV).astype(F32)

    def masked(at, count):
        deep = deep_ref[at : at + count, :].astype(F32)
        keep = level < jnp.concatenate([deep, deep], axis=1)
        return jnp.where(keep, cot_ref[at : at + count, :].astype(F32), 0.0)

    for y in range(ROWS):
        line = dep_ref[y : y + 1, :].astype(F32)
        deep_ref[y * COLS : (y + 1) * COLS, :] = dot((eye * line).astype(BF16), ones).astype(BF16)
    for out_ref, first in ((top_ref, ROWS - 2), (low_ref, 0)):
        at = first * COLS
        out_ref[:, 0:CH] = field_ref[at : at + 2 * COLS, :]
        out_ref[:, CH : 2 * CH] = masked(at, 2 * COLS).astype(BF16)
        out_ref[:, 2 * CH : LANES] = deep_ref[at : at + 2 * COLS, :]
    for out_ref, column, skip in ((west_ref, 0, 0), (east_ref, COLS - 16, 14)):
        for y in range(ROWS):
            at = y * COLS + column
            cells = slice(2 * y, 2 * y + 2)
            edge[cells, 0:CH] = field_ref[at : at + 16, :].astype(F32)[skip : skip + 2]
            edge[cells, CH : 2 * CH] = masked(at, 16)[skip : skip + 2]
            edge[cells, 2 * CH : LANES] = deep_ref[at : at + 16, :].astype(F32)[skip : skip + 2]
        out_ref[...] = edge[...].astype(BF16)


def strip_kernel(
    scal_ref, top_ref, low_ref, west_ref, east_ref, near_ref, far_ref, upper_ref, lower_ref, fold_ref, west, east, far,
    extra, strip,
):
    west[...] = west_ref[...].astype(F32)
    east[...] = east_ref[...].astype(F32)
    far[...] = far_ref[...].astype(F32)
    strip[...] = jnp.zeros(strip.shape, F32)
    for out_ref, rows_ref, first in ((upper_ref, top_ref, ROWS - 2), (lower_ref, low_ref, 0)):
        for k in range(2):
            y, at = first + k, k * PITCH
            strip[at : at + COLS, :] = rows_ref[k * COLS : (k + 1) * COLS, :].astype(F32)
            strip[at + 64 : at + 66, :] = east[2 * y : 2 * y + 2, :]
            strip[at + 70 : at + 72, :] = west[2 * y : 2 * y + 2, :]
        out_ref[...] = strip[...].astype(BF16)
    to = lax.broadcasted_iota(jnp.int32, (PITCH, 144), 0)
    at = lax.broadcasted_iota(jnp.int32, (PITCH, 144), 1)
    want = 63 - jnp.where(to >= 70, to - PITCH, to) + scal_ref[1]
    want = jnp.where((to >= 66) & (to < 70), -98, want)
    have = jnp.where(at < 128, at, jnp.where(at < 130, at - 130, jnp.where(at < 132, at - 2, -99)))
    pick = (want == have).astype(F32).astype(BF16)
    extra[...] = jnp.zeros(extra.shape, F32)
    for j in range(2):
        i = 1 - j
        y = ROWS - 2 + i
        extra[0:2, :] = west[2 * y : 2 * y + 2, :]
        extra[2:4, :] = far[2 * i : 2 * i + 2, :]
        rows = slice(i * COLS, (i + 1) * COLS)
        cells = jnp.concatenate([top_ref[rows, :], near_ref[rows, :], extra[...].astype(BF16)], axis=0)
        strip[j * PITCH : (j + 1) * PITCH, :] = dot(pick, cells)
    fold_ref[...] = strip[...].astype(BF16)


def first_kernel(
    scal_ref, field_ref, cot_ref, dep_ref, west_ref, east_ref, south_ref, north_ref, fold_ref,
    w_ref, bias_ref,
    pf_ref, pd_ref, ph_ref, slope_ref, keep_ref, send_ref,
    ext, depth, west, east, south, north, back,
):
    top = scal_ref[0] == 1
    west[...] = west_ref[...].astype(F32)
    east[...] = east_ref[...].astype(F32)
    south[...] = south_ref[...].astype(F32)
    north[...] = north_ref[...].astype(F32) + fold_ref[...].astype(F32)

    def fill(out_ref, lanes, own, width, head):
        if head:
            out_ref[0:head, :] = jnp.zeros((head, width), F32)
        for g in range(21):
            base = head + g * PITCH
            out_ref[base : base + 8, :] = jnp.zeros((8, width), F32)
            y = g - 3
            if 0 <= y < 16:
                out_ref[base : base + 2, :] = east[2 * y : 2 * y + 2, lanes]
            elif -2 <= y < 0:
                at = (y + 2) * PITCH + 64
                out_ref[base : base + 2, :] = south[at : at + 2, lanes]
            elif y >= 16:
                at = (y - 16) * PITCH + 64
                out_ref[base : base + 2, :] = north[at : at + 2, lanes]
            y = g - 2
            if 0 <= y < 16:
                out_ref[base + 6 : base + 8, :] = west[2 * y : 2 * y + 2, lanes]
            elif -2 <= y < 0:
                at = (y + 2) * PITCH + 70
                out_ref[base + 6 : base + 8, :] = south[at : at + 2, lanes]
            elif 16 <= y < 18:
                at = (y - 16) * PITCH + 70
                out_ref[base + 6 : base + 8, :] = north[at : at + 2, lanes]
        for y in range(-2, 18):
            base = head + (y + 2) * PITCH + 8
            if y < 0:
                out_ref[base : base + 64, :] = south[(y + 2) * PITCH : (y + 2) * PITCH + 64, lanes]
            elif y < 16:
                out_ref[base : base + 64, :] = own(y)
            else:
                out_ref[base : base + 64, :] = north[(y - 16) * PITCH : (y - 16) * PITCH + 64, lanes]
        tail = head + 20 * PITCH + 8
        rest = out_ref.shape[0] - tail
        if rest:
            out_ref[tail:, :] = jnp.zeros((rest, width), F32)

    level = lax.broadcasted_iota(jnp.int32, (1, CH), 1) % LEV
    level = level.astype(F32)

    def wet(values):
        return level < jnp.concatenate([values, values], axis=1)

    def own_field(y):
        return field_ref[y * 64 : (y + 1) * 64, :].astype(F32)

    def own_depth(y):
        return dep_ref[y * 64 : (y + 1) * 64, :].astype(F32)

    def own_delta(y):
        cells = cot_ref[y * 64 : (y + 1) * 64, :].astype(F32)
        return jnp.where(wet(own_depth(y)), cells, 0.0)

    fill(ext, slice(0, CH), own_field, CH, HEAD)
    fill(depth, slice(2 * CH, LANES), own_depth, 128, 0)
    shifted(pf_ref, ext, EXT)
    fill(ext, slice(CH, 2 * CH), own_delta, CH, HEAD)
    shifted(pd_ref, ext, EXT)

    bias = bias_ref[...]

    def finish(pre, p):
        count = pre.shape[0]
        x = pre + bias
        square = x * x
        t = jnp.tanh(C0 * (x + C1 * (square * x)))
        keep = wet(depth[p : p + count, :])
        half = 0.5 * (1.0 + t)
        hidden = jnp.where(keep, x * half, 0.0).astype(BF16).astype(F32)
        slope = half + (0.5 * C0) * x * (1.0 - t * t) * (1.0 + (3.0 * C1) * square)
        return hidden, jnp.where(keep, slope, 0.0)

    first = 72
    step = 176
    for start in range(first, first + 1232, step):
        hidden, slope = finish(taps(pf_ref, start - PITCH, step, w_ref, plain(), False), start)
        ext[HEAD + start - first : HEAD + start - first + step, :] = hidden
        slope_ref[start - first : start - first + step, :] = slope
    start = 1296
    picks = [(a, [jnp.where(top, 8 - 3 * a - b, 3 * a + b) for b in range(3)]) for a in range(3)]
    hidden, slope = finish(taps(pf_ref, start - PITCH, 80, w_ref, picks, False), start)
    at = start - first
    beyond = lax.broadcasted_iota(jnp.int32, (8, CH), 0) >= 4
    ext[HEAD + at : HEAD + at + 8, :] = jnp.where(beyond, hidden[:8], ext[HEAD + at : HEAD + at + 8, :])
    slope_ref[at : at + 8, :] = jnp.where(beyond, slope[:8], slope_ref[at : at + 8, :])
    ext[HEAD + at + 8 : HEAD + at + 80, :] = hidden[8:]
    slope_ref[at + 8 : at + 80, :] = slope[8:]
    ext[HEAD + MID : HEAD + MID + 8, :] = jnp.zeros((8, CH), F32)
    shifted(ph_ref, ext, MID)
    transposed_own(pd_ref, 144, back)
    weight_grad(keep_ref, send_ref, scal_ref[2], back, ph_ref, 0)


def second_kernel(
    scal_ref, pd_ref, pf_ref, slope_ref, w_ref, pe_ref, keep_ref, send_ref, ext, back
):
    top = scal_ref[0] == 1
    first = 72
    ext[0:HEAD, :] = jnp.zeros((HEAD, CH), F32)
    ext[HEAD + MID : HEAD + MID + 8, :] = jnp.zeros((8, CH), F32)

    def put(sums, p):
        at = p - first
        count = sums.shape[0]
        delta = (slope_ref[at : at + count, :] * sums).astype(BF16).astype(F32)
        ext[HEAD + at : HEAD + at + count, :] = delta

    step = 232
    for start in range(first, first + 1160, step):
        put(taps(pd_ref, start - PITCH, step, w_ref, turned(), True), start)
    start = 1232
    sums = taps(pd_ref, start - PITCH, 144, w_ref, turned((0,)), True)
    over = [(2, [jnp.where(top, 6 + b, 2 - b) for b in range(3)])]
    sums = sums + taps(pd_ref, start - PITCH, 144, w_ref, over, True)
    middle = taps(pd_ref, start - PITCH, 72, w_ref, turned((1,)), True)
    beside = [(1, [jnp.where(top, 3 + b, 5 - b) for b in range(3)])]
    upper = taps(pd_ref, 1296 - PITCH, 80, w_ref, beside, True)
    beyond = lax.broadcasted_iota(jnp.int32, (8, CH), 0) >= 4
    put(sums[:64] + middle[:64], 1232)
    put(sums[64:72] + jnp.where(beyond, upper[:8], middle[64:]), 1296)
    put(sums[72:] + upper[8:], 1304)
    start = 1224
    gap = taps(pd_ref, start - PITCH, 16, w_ref, turned((0, 1)), True)
    gap = gap + taps(pd_ref, start - PITCH, 16, w_ref, over, True)
    at = start - first
    delta = (slope_ref[at : at + 8, :] * gap[:8]).astype(BF16).astype(F32)
    ext[HEAD + at : HEAD + at + 8, :] = jnp.where(beyond, delta, ext[HEAD + at : HEAD + at + 8, :])
    shifted(pe_ref, ext, MID)
    transposed_own(pe_ref, 72, back)
    weight_grad(keep_ref, send_ref, scal_ref[2], back, pf_ref, 72)


def third_kernel(
    scal_ref, ph_ref, pe_ref, field_ref, cot_ref, dep_ref, w1_ref, w2_ref, bias_ref, out_ref, in_ref
):
    top = scal_ref[0] == 1
    level = (lax.broadcasted_iota(jnp.int32, (1, CH), 1) % LEV).astype(F32)
    bias = bias_ref[...]

    def wet(at):
        deep = dep_ref[at, :].astype(F32)
        return level < jnp.concatenate([deep, deep], axis=1)

    for y in range(0, 16, 4):
        p = 144 + y * PITCH
        sums = taps(ph_ref, p - 144, 4 * PITCH, w2_ref, plain(), False)
        for k in range(4):
            at = slice((y + k) * 64, (y + k + 1) * 64)
            cells = field_ref[at, :].astype(F32) + sums[k * PITCH + 8 : (k + 1) * PITCH] + bias
            out_ref[at, :] = jnp.where(wet(at), cells, 0.0).astype(BF16)

    def put(cells, y):
        at = slice(y * 64, (y + 1) * 64)
        total = jnp.where(wet(at), cot_ref[at, :].astype(F32), 0.0) + cells
        in_ref[at, :] = total.astype(BF16)

    for y in range(0, 15, 5):
        p = 144 + y * PITCH
        sums = taps(pe_ref, p - 144, 5 * PITCH, w1_ref, turned(), True)
        for k in range(5):
            put(sums[k * PITCH + 8 : (k + 1) * PITCH], y + k)
    p = 144 + 15 * PITCH + 8
    over = [(2, [jnp.where(top, 6 + b, 2 - b) for b in range(3)])]
    sums = taps(pe_ref, p - 144, 64, w1_ref, turned((0, 1)), True)
    put(sums + taps(pe_ref, p - 144, 64, w1_ref, over, True), 15)


def last_kernel(scal_ref, mine_ref, other_ref, one_ref, two_ref):
    first = scal_ref[2] == 0
    down = lax.broadcasted_iota(jnp.int32, (CH, CH), 0)
    across = lax.broadcasted_iota(jnp.int32, (CH, CH), 1)
    eye = jnp.where(down == across, SCALE, 0.0).astype(BF16)
    for k in range(18):
        mine = mine_ref[:, k * CH : (k + 1) * CH]
        other = other_ref[:, k * CH : (k + 1) * CH]
        low, high = jnp.where(first, mine, other), jnp.where(first, other, mine)
        kernel = dot(eye, jnp.concatenate([low, high], axis=0), ((1,), (1,)))
        out_ref, at = (one_ref, k) if k < 9 else (two_ref, k - 9)
        out_ref[at * CH : (at + 1) * CH, :] = kernel


VM = pl.BlockSpec(memory_space=pltpu.VMEM)
SM = pl.BlockSpec(memory_space=pltpu.SMEM)


def call(body, outs, scratch, *args, flops=10**7, scalars=True):
    moved = sum(math.prod(a.shape) * a.dtype.itemsize for a in args)
    moved += sum(math.prod(s) * jnp.dtype(t).itemsize for s, t in outs)
    return pl.pallas_call(
        body,
        cost_estimate=pl.CostEstimate(flops=flops, bytes_accessed=moved, transcendentals=0),
        out_shape=[jax.ShapeDtypeStruct(s, t) for s, t in outs],
        in_specs=([SM] if scalars else [VM]) + [VM] * (len(args) - 1),
        out_specs=[VM] * len(outs),
        scratch_shapes=scratch,
        compiler_params=pltpu.CompilerParams(vmem_limit_bytes=24 << 20),
    )(*args)


def block(
    field, weight_one, bias_one, weight_two, bias_two, depth_levels, fold_partner, cotangent
):
    n_low = lax.axis_size("z")
    n_high = lax.axis_size("yl") * lax.axis_size("x")
    n_z, n_m = n_low * n_high, 4
    merid = lax.axis_index(MERID)
    core = lax.axis_index("c")
    flat_field = field.reshape(ROWS * COLS, CH)
    flat_cot = cotangent.reshape(ROWS * COLS, CH)
    edge, rim = ((2 * ROWS, LANES), BF16), ((2 * COLS, LANES), BF16)
    flat_deep, top_rows, low_rows, west_edge, east_edge = call(
        pack_kernel,
        [((ROWS * COLS, 128), BF16), rim, rim, edge, edge],
        [pltpu.VMEM((2 * ROWS, LANES), F32)],
        flat_field, flat_cot, depth_levels, scalars=False,
    )

    fold_partner, west_edge = lax.optimization_barrier((fold_partner, west_edge))
    shift = (fold_partner[0] + 1) % (n_z * COLS)
    quotient, rest = shift // COLS, shift % COLS
    scal = jnp.stack([(merid == n_m - 1).astype(jnp.int32), rest.astype(jnp.int32), core.astype(jnp.int32)])

    def hop(rows, target):
        route = [(m * n_m + n_m - 1, (target(m) % n_z) * n_m + n_m - 1) for m in range(n_z)]
        return lax.ppermute(rows, ZONAL + MERID, route)

    near = hop(top_rows, lambda m: m - 1)
    far = hop(west_edge[2 * ROWS - 4 :], lambda m: m - 2)
    west = lax.ppermute(east_edge, ZONAL, [(i, (i + 1) % n_z) for i in range(n_z)])
    east = lax.ppermute(west_edge, ZONAL, [((i + 1) % n_z, i) for i in range(n_z)])
    strip = ((2 * PITCH, LANES), BF16)
    upper, lower, fold = call(
        strip_kernel,
        [strip, strip, strip],
        [
            pltpu.VMEM((2 * ROWS, LANES), F32),
            pltpu.VMEM((2 * ROWS, LANES), F32),
            pltpu.VMEM((4, LANES), F32),
            pltpu.VMEM((16, LANES), F32),
            pltpu.VMEM((2 * PITCH, LANES), F32),
        ],
        scal, top_rows, low_rows, west, east, near, far,
    )
    south = lax.ppermute(upper, MERID, [(i, i + 1) for i in range(n_m - 1)])
    north = lax.ppermute(lower, MERID, [(i + 1, i) for i in range(n_m - 1)])

    def turn(rows, high):
        return hop(rows, lambda m: n_low * ((n_high - 1 - m // n_low + high) % n_high) + m % n_low)

    def slide(rows, low):
        return hop(rows, lambda m: n_low * (m // n_low) + n_low - 1 + low - m % n_low)

    fold = lax.switch(quotient // n_low, [lambda rows, h=h: turn(rows, h) for h in range(n_high)], fold)
    fold = lax.switch(quotient % n_low, [lambda rows, h=h: slide(rows, h) for h in range(n_low)], fold)
    w1 = weight_one.reshape(9, CH, CH)
    w2 = weight_two.reshape(9, CH, CH)
    half = ((CH // 2, 9 * CH), F32)
    pf, pd, ph, slope, keep_two, send_two = call(
        first_kernel,
        [((EXT, 3 * CH), BF16), ((EXT, 3 * CH), BF16), ((MID, 3 * CH), BF16), ((MID, CH), F32), half, half],
        [
            pltpu.VMEM((EXT + 16, CH), F32),
            pltpu.VMEM((EXT, 128), F32),
            pltpu.VMEM((32, LANES), F32),
            pltpu.VMEM((32, LANES), F32),
            pltpu.VMEM((2 * PITCH, LANES), F32),
            pltpu.VMEM((2 * PITCH, LANES), F32),
            pltpu.VMEM((CH, INNER), BF16),
        ],
        scal, flat_field, flat_cot, flat_deep, west, east, south, north, fold, w1, bias_one.reshape(1, CH),
        flops=3 * 10**9,
    )
    swap = [(0, 1), (1, 0)]
    came_two = lax.ppermute(send_two, "c", swap)
    pe, keep_one, send_one = call(
        second_kernel,
        [((MID, 3 * CH), BF16), half, half],
        [pltpu.VMEM((MID + 16, CH), F32), pltpu.VMEM((CH, INNER), BF16)],
        scal, pd, pf, slope, w2,
        flops=3 * 10**9,
    )
    came_one = lax.ppermute(send_one, "c", swap)
    output, input_grad = call(
        third_kernel,
        [((ROWS * COLS, CH), BF16), ((ROWS * COLS, CH), BF16)],
        [],
        scal, ph, pe, flat_field, flat_cot, flat_deep, w1, w2, bias_two.reshape(1, CH),
        flops=3 * 10**9,
    )

    n_p = lax.axis_size("yl") * lax.axis_size("x") * lax.axis_size("yh")
    rows = CH // 2 // n_p
    width = 18 * CH
    sums = jnp.concatenate([keep_one + came_one, keep_two + came_two], axis=1).astype(BF16)
    sums = lax.all_to_all(sums.reshape(n_p, rows, width), PLANE, 0, 0)
    sums = jnp.sum(sums.astype(F32), axis=0)
    part = rows // n_low
    sums = lax.all_to_all(sums.reshape(n_low, part * 36, 128), "z", 0, 0)
    piece = jnp.sum(sums, axis=0).astype(BF16)
    line = lax.all_to_all(jnp.broadcast_to(piece[None], (n_low, part * 36, 128)), "z", 0, 0)
    line = line.reshape(rows, width)
    mine = lax.all_to_all(jnp.broadcast_to(line[None], (n_p, rows, width)), PLANE, 0, 0)
    mine = mine.reshape(CH // 2, width)
    other = lax.ppermute(mine, "c", swap)
    grad_one, grad_two = call(
        last_kernel,
        [((9 * CH, CH), F32), ((9 * CH, CH), F32)],
        [],
        scal, mine, other,
    )
    return (
        output.reshape(ROWS, COLS, CH),
        input_grad.reshape(ROWS, COLS, CH),
        grad_one.reshape(3, 3, CH, CH),
        grad_two.reshape(3, 3, CH, CH),
    )


def solution(mesh):
    fine = Mesh(mesh.devices.reshape(SPLIT + (2, 2)), ZONAL + MERID)
    cells = P(MERID, ZONAL, None)
    return jax.shard_map(
        block,
        mesh=fine,
        in_specs=(cells, P(), P(), P(), P(), P(MERID, ZONAL), P(), cells),
        out_specs=(cells, cells, P(), P()),
        check_vma=False,
    )
```

```python
import math

import jax
import jax.numpy as jnp
from jax import lax
from jax.experimental import pallas as pl
from jax.experimental.pallas import tpu as pltpu
from jax.sharding import Mesh
from jax.sharding import PartitionSpec as P


LEV = 64
SPLIT = (2, 4, 8)
ZONAL = ("yl", "x", "z")
MERID = ("yh", "c")
PLANE = ("yl", "x", "yh")
SCALE = 1.0 / 512.0
ROWS = 16
COLS = 64
CH = 256
PITCH = 72
EXT = 20 * PITCH + 16
MID = 18 * PITCH + 8
INNER = 16 * PITCH
LANES = 2 * CH + 128
HEAD = 8
F32 = jnp.float32
BF16 = jnp.bfloat16
C0 = math.sqrt(2.0 / math.pi)
C1 = 0.044715


def dot(a, b, dims=((1,), (0,))):
    return lax.dot_general(a, b, (dims, ((), ())), preferred_element_type=F32)


def taps(lhs_ref, row, count, w_ref, picks, transposed):
    total = None
    for a, indices in picks:
        lhs = lhs_ref[row + a * PITCH : row + a * PITCH + count, :]
        side = jnp.concatenate([w_ref[k] for k in indices], axis=1 if transposed else 0)
        part = dot(lhs, side, ((1,), (1 if transposed else 0,)))
        total = part if total is None else total + part
    return total


def plain(rows_of=(0, 1, 2)):
    return [(a, [3 * a + b for b in range(3)]) for a in rows_of]


def turned(rows_of=(0, 1, 2)):
    return [(a, [8 - 3 * a - b for b in range(3)]) for a in rows_of]


def shifted(out_ref, src_ref, count):
    step = 112
    for start in range(0, count, step):
        size = min(step, count - start)
        for b in range(3):
            at = HEAD + start + b - 1
            out_ref[start : start + size, b * CH : (b + 1) * CH] = src_ref[at : at + size, :].astype(BF16)


def own_cells(count, first):
    place = (lax.broadcasted_iota(jnp.int32, (count, CH), 0) + first) % PITCH
    return place >= 8


def transposed_own(ref, first, out_ref):
    eye = (
        lax.broadcasted_iota(jnp.int32, (CH, CH), 0) == lax.broadcasted_iota(jnp.int32, (CH, CH), 1)
    ).astype(BF16)
    step = 128
    for start in range(0, INNER, step):
        cells = ref[first + start : first + start + step, CH : 2 * CH].astype(F32)
        cells = jnp.where(own_cells(step, start), cells, 0.0).astype(BF16)
        out_ref[:, start : start + step] = dot(eye, cells, ((1,), (1,))).astype(BF16)


def weight_grad(keep_ref, send_ref, core, turned_ref, patches_ref, row):
    for a in range(3):
        for b in range(3):
            cells = patches_ref[row + a * PITCH : row + a * PITCH + INNER, b * CH : (b + 1) * CH]
            at = (3 * a + b) * CH
            sums = dot(turned_ref[...], cells)
            low, high = sums[: CH // 2], sums[CH // 2 :]
            keep_ref[:, at : at + CH] = jnp.where(core == 0, low, high)
            send_ref[:, at : at + CH] = jnp.where(core == 0, high, low)


def pack_kernel(
    field_far, cot_far, dep_far, deep_ref, top_ref, low_ref, west_ref, east_ref, far_ref,
    edge, field_ref, cot_ref, dep_ref, sems,
):
    copies = [
        pltpu.make_async_copy(dep_far, dep_ref, sems.at[0]),
        pltpu.make_async_copy(field_far, field_ref, sems.at[1]),
        pltpu.make_async_copy(cot_far, cot_ref, sems.at[2]),
    ]
    for copy in copies:
        copy.start()
    copies[0].wait()
    eye = (
        lax.broadcasted_iota(jnp.int32, (COLS, COLS), 0) == lax.broadcasted_iota(jnp.int32, (COLS, COLS), 1)
    ).astype(F32)
    ones = jnp.ones((COLS, 128), BF16)
    level = (lax.broadcasted_iota(jnp.int32, (1, CH), 1) % LEV).astype(F32)

    def masked(at, count):
        deep = deep_ref[at : at + count, :].astype(F32)
        keep = level < jnp.concatenate([deep, deep], axis=1)
        return jnp.where(keep, cot_ref[at : at + count, :].astype(F32), 0.0)

    for y in range(ROWS):
        line = dep_ref[y : y + 1, :].astype(F32)
        deep_ref[y * COLS : (y + 1) * COLS, :] = dot((eye * line).astype(BF16), ones).astype(BF16)
    copies[1].wait()
    copies[2].wait()
    for out_ref, first in ((top_ref, ROWS - 2), (low_ref, 0)):
        at = first * COLS
        out_ref[:, 0:CH] = field_ref[at : at + 2 * COLS, :]
        out_ref[:, CH : 2 * CH] = masked(at, 2 * COLS).astype(BF16)
        out_ref[:, 2 * CH : LANES] = deep_ref[at : at + 2 * COLS, :]
    for out_ref, column, skip in ((west_ref, 0, 0), (east_ref, COLS - 16, 14)):
        for y in range(ROWS):
            at = y * COLS + column
            cells = slice(2 * y, 2 * y + 2)
            edge[cells, 0:CH] = field_ref[at : at + 16, :].astype(F32)[skip : skip + 2]
            edge[cells, CH : 2 * CH] = masked(at, 16)[skip : skip + 2]
            edge[cells, 2 * CH : LANES] = deep_ref[at : at + 16, :].astype(F32)[skip : skip + 2]
        out_ref[...] = edge[...].astype(BF16)
        if skip == 0:
            far_ref[...] = edge[2 * ROWS - 4 : 2 * ROWS, :].astype(BF16)


def strip_kernel(
    scal_ref, top_ref, low_ref, west_ref, east_ref, near_ref, far_ref, upper_ref, lower_ref, fold_ref, west, east, far,
    extra, strip,
):
    west[...] = west_ref[...].astype(F32)
    east[...] = east_ref[...].astype(F32)
    far[...] = far_ref[...].astype(F32)
    strip[...] = jnp.zeros(strip.shape, F32)
    for out_ref, rows_ref, first in ((upper_ref, top_ref, ROWS - 2), (lower_ref, low_ref, 0)):
        for k in range(2):
            y, at = first + k, k * PITCH
            strip[at : at + COLS, :] = rows_ref[k * COLS : (k + 1) * COLS, :].astype(F32)
            strip[at + 64 : at + 66, :] = east[2 * y : 2 * y + 2, :]
            strip[at + 70 : at + 72, :] = west[2 * y : 2 * y + 2, :]
        out_ref[...] = strip[...].astype(BF16)
    to = lax.broadcasted_iota(jnp.int32, (PITCH, 144), 0)
    at = lax.broadcasted_iota(jnp.int32, (PITCH, 144), 1)
    want = 63 - jnp.where(to >= 70, to - PITCH, to) + scal_ref[1]
    want = jnp.where((to >= 66) & (to < 70), -98, want)
    have = jnp.where(at < 128, at, jnp.where(at < 130, at - 130, jnp.where(at < 132, at - 2, -99)))
    pick = (want == have).astype(F32).astype(BF16)
    extra[...] = jnp.zeros(extra.shape, F32)
    here = lax.broadcasted_iota(jnp.int32, (PITCH, 128), 0) == lax.broadcasted_iota(jnp.int32, (PITCH, 128), 1)
    third = lax.broadcasted_iota(jnp.int32, (8, 128), 0) == 2
    for j in range(2):
        i = 1 - j
        y = ROWS - 2 + i
        extra[0:2, :] = west[2 * y : 2 * y + 2, :]
        extra[2:4, :] = far[2 * i : 2 * i + 2, :]
        rows = slice(i * COLS, (i + 1) * COLS)
        cells = jnp.concatenate([top_ref[rows, :], near_ref[rows, :], extra[...].astype(BF16)], axis=0)
        cells = dot(pick, cells)
        fold_ref[j * PITCH : (j + 1) * PITCH, :] = cells[:, : 2 * CH].astype(BF16)
        line = jnp.sum(jnp.where(here, cells[:, 2 * CH :], 0.0), axis=0, keepdims=True)
        free = slice(j * PITCH + COLS, j * PITCH + COLS + 8)
        tile = jnp.where(third, jnp.broadcast_to(line, (8, 128)), cells[COLS:, :128])
        fold_ref[free, 0:128] = tile.astype(BF16)


def first_kernel(
    scal_ref, field_ref, cot_ref, dep_ref, west_ref, east_ref, south_ref, north_ref, fold_ref,
    w_far, bias_ref,
    pf_ref, pd_ref, ph_far, slope_ref, keep_ref, send_ref,
    ext, depth, west, east, south, north, back, w_ref, ph_ref, sems,
):
    weights = pltpu.make_async_copy(w_far, w_ref, sems.at[0])
    weights.start()
    top = scal_ref[0] == 1
    west[...] = west_ref[...].astype(F32)
    east[...] = east_ref[...].astype(F32)
    south[...] = south_ref[...].astype(F32)
    north[:, 0 : 2 * CH] = north_ref[:, 0 : 2 * CH].astype(F32) + fold_ref[...].astype(F32)
    here = lax.broadcasted_iota(jnp.int32, (PITCH, 128), 0) == lax.broadcasted_iota(jnp.int32, (PITCH, 128), 1)
    for j in range(2):
        tile = fold_ref[j * PITCH + COLS : j * PITCH + COLS + 8, 0:128].astype(F32)
        spread = jnp.where(here, jnp.broadcast_to(tile[2:3, :], (PITCH, 128)), 0.0).astype(BF16)
        rows = slice(j * PITCH, (j + 1) * PITCH)
        north[rows, 2 * CH :] = north_ref[rows, 2 * CH :].astype(F32) + dot(spread, jnp.ones((128, 128), BF16))

    def fill(out_ref, lanes, own, width, head):
        if head:
            out_ref[0:head, :] = jnp.zeros((head, width), F32)
        for g in range(21):
            base = head + g * PITCH
            out_ref[base : base + 8, :] = jnp.zeros((8, width), F32)
            y = g - 3
            if 0 <= y < 16:
                out_ref[base : base + 2, :] = east[2 * y : 2 * y + 2, lanes]
            elif -2 <= y < 0:
                at = (y + 2) * PITCH + 64
                out_ref[base : base + 2, :] = south[at : at + 2, lanes]
            elif y >= 16:
                at = (y - 16) * PITCH + 64
                out_ref[base : base + 2, :] = north[at : at + 2, lanes]
            y = g - 2
            if 0 <= y < 16:
                out_ref[base + 6 : base + 8, :] = west[2 * y : 2 * y + 2, lanes]
            elif -2 <= y < 0:
                at = (y + 2) * PITCH + 70
                out_ref[base + 6 : base + 8, :] = south[at : at + 2, lanes]
            elif 16 <= y < 18:
                at = (y - 16) * PITCH + 70
                out_ref[base + 6 : base + 8, :] = north[at : at + 2, lanes]
        for y in range(-2, 18):
            base = head + (y + 2) * PITCH + 8
            if y < 0:
                out_ref[base : base + 64, :] = south[(y + 2) * PITCH : (y + 2) * PITCH + 64, lanes]
            elif y < 16:
                out_ref[base : base + 64, :] = own(y)
            else:
                out_ref[base : base + 64, :] = north[(y - 16) * PITCH : (y - 16) * PITCH + 64, lanes]
        tail = head + 20 * PITCH + 8
        rest = out_ref.shape[0] - tail
        if rest:
            out_ref[tail:, :] = jnp.zeros((rest, width), F32)

    level = lax.broadcasted_iota(jnp.int32, (1, CH), 1) % LEV
    level = level.astype(F32)

    def wet(values):
        return level < jnp.concatenate([values, values], axis=1)

    def own_field(y):
        return field_ref[y * 64 : (y + 1) * 64, :].astype(F32)

    def own_depth(y):
        return dep_ref[y * 64 : (y + 1) * 64, :].astype(F32)

    def own_delta(y):
        cells = cot_ref[y * 64 : (y + 1) * 64, :].astype(F32)
        return jnp.where(wet(own_depth(y)), cells, 0.0)

    fill(ext, slice(0, CH), own_field, CH, HEAD)
    fill(depth, slice(2 * CH, LANES), own_depth, 128, 0)
    shifted(pf_ref, ext, EXT)
    fill(ext, slice(CH, 2 * CH), own_delta, CH, HEAD)
    shifted(pd_ref, ext, EXT)

    bias = bias_ref[...]
    weights.wait()

    def finish(pre, p):
        count = pre.shape[0]
        x = pre + bias
        square = x * x
        t = jnp.tanh(C0 * (x + C1 * (square * x)))
        keep = wet(depth[p : p + count, :])
        half = 0.5 * (1.0 + t)
        hidden = jnp.where(keep, x * half, 0.0).astype(BF16).astype(F32)
        slope = half + (0.5 * C0) * x * (1.0 - t * t) * (1.0 + (3.0 * C1) * square)
        return hidden, jnp.where(keep, slope, 0.0)

    first = 72
    step = 176
    for start in range(first, first + 1232, step):
        hidden, slope = finish(taps(pf_ref, start - PITCH, step, w_ref, plain(), False), start)
        ext[HEAD + start - first : HEAD + start - first + step, :] = hidden
        slope_ref[start - first : start - first + step, :] = slope
    start = 1296
    picks = [(a, [jnp.where(top, 8 - 3 * a - b, 3 * a + b) for b in range(3)]) for a in range(3)]
    hidden, slope = finish(taps(pf_ref, start - PITCH, 80, w_ref, picks, False), start)
    at = start - first
    beyond = lax.broadcasted_iota(jnp.int32, (8, CH), 0) >= 4
    ext[HEAD + at : HEAD + at + 8, :] = jnp.where(beyond, hidden[:8], ext[HEAD + at : HEAD + at + 8, :])
    slope_ref[at : at + 8, :] = jnp.where(beyond, slope[:8], slope_ref[at : at + 8, :])
    ext[HEAD + at + 8 : HEAD + at + 80, :] = hidden[8:]
    slope_ref[at + 8 : at + 80, :] = slope[8:]
    ext[HEAD + MID : HEAD + MID + 8, :] = jnp.zeros((8, CH), F32)
    shifted(ph_ref, ext, MID)
    leave = pltpu.make_async_copy(ph_ref, ph_far, sems.at[1])
    leave.start()
    transposed_own(pd_ref, 144, back)
    weight_grad(keep_ref, send_ref, scal_ref[2], back, ph_ref, 0)
    leave.wait()


def second_kernel(
    scal_ref, pd_ref, pf_ref, slope_ref, w_ref, pe_far, keep_ref, send_ref, ext, back, pe_ref, sem
):
    top = scal_ref[0] == 1
    first = 72
    ext[0:HEAD, :] = jnp.zeros((HEAD, CH), F32)
    ext[HEAD + MID : HEAD + MID + 8, :] = jnp.zeros((8, CH), F32)

    def put(sums, p):
        at = p - first
        count = sums.shape[0]
        delta = (slope_ref[at : at + count, :] * sums).astype(BF16).astype(F32)
        ext[HEAD + at : HEAD + at + count, :] = delta

    step = 232
    for start in range(first, first + 1160, step):
        put(taps(pd_ref, start - PITCH, step, w_ref, turned(), True), start)
    start = 1232
    sums = taps(pd_ref, start - PITCH, 144, w_ref, turned((0,)), True)
    over = [(2, [jnp.where(top, 6 + b, 2 - b) for b in range(3)])]
    sums = sums + taps(pd_ref, start - PITCH, 144, w_ref, over, True)
    middle = taps(pd_ref, start - PITCH, 72, w_ref, turned((1,)), True)
    beside = [(1, [jnp.where(top, 3 + b, 5 - b) for b in range(3)])]
    upper = taps(pd_ref, 1296 - PITCH, 80, w_ref, beside, True)
    beyond = lax.broadcasted_iota(jnp.int32, (8, CH), 0) >= 4
    put(sums[:64] + middle[:64], 1232)
    put(sums[64:72] + jnp.where(beyond, upper[:8], middle[64:]), 1296)
    put(sums[72:] + upper[8:], 1304)
    start = 1224
    gap = taps(pd_ref, start - PITCH, 16, w_ref, turned((0, 1)), True)
    gap = gap + taps(pd_ref, start - PITCH, 16, w_ref, over, True)
    at = start - first
    delta = (slope_ref[at : at + 8, :] * gap[:8]).astype(BF16).astype(F32)
    ext[HEAD + at : HEAD + at + 8, :] = jnp.where(beyond, delta, ext[HEAD + at : HEAD + at + 8, :])
    shifted(pe_ref, ext, MID)
    leave = pltpu.make_async_copy(pe_ref, pe_far, sem)
    leave.start()
    transposed_own(pe_ref, 72, back)
    weight_grad(keep_ref, send_ref, scal_ref[2], back, pf_ref, 72)
    leave.wait()


def third_kernel(
    scal_ref, ph_ref, pe_ref, field_ref, cot_ref, dep_ref, w1_ref, w2_ref, bias_ref, out_ref, in_ref
):
    top = scal_ref[0] == 1
    level = (lax.broadcasted_iota(jnp.int32, (1, CH), 1) % LEV).astype(F32)
    bias = bias_ref[...]

    def wet(at):
        deep = dep_ref[at, :].astype(F32)
        return level < jnp.concatenate([deep, deep], axis=1)

    for y in range(0, 16, 4):
        p = 144 + y * PITCH
        sums = taps(ph_ref, p - 144, 4 * PITCH, w2_ref, plain(), False)
        for k in range(4):
            at = slice((y + k) * 64, (y + k + 1) * 64)
            cells = field_ref[at, :].astype(F32) + sums[k * PITCH + 8 : (k + 1) * PITCH] + bias
            out_ref[at, :] = jnp.where(wet(at), cells, 0.0).astype(BF16)

    def put(cells, y):
        at = slice(y * 64, (y + 1) * 64)
        total = jnp.where(wet(at), cot_ref[at, :].astype(F32), 0.0) + cells
        in_ref[at, :] = total.astype(BF16)

    for y in range(0, 15, 5):
        p = 144 + y * PITCH
        sums = taps(pe_ref, p - 144, 5 * PITCH, w1_ref, turned(), True)
        for k in range(5):
            put(sums[k * PITCH + 8 : (k + 1) * PITCH], y + k)
    p = 144 + 15 * PITCH + 8
    over = [(2, [jnp.where(top, 6 + b, 2 - b) for b in range(3)])]
    sums = taps(pe_ref, p - 144, 64, w1_ref, turned((0, 1)), True)
    put(sums + taps(pe_ref, p - 144, 64, w1_ref, over, True), 15)


def last_kernel(scal_ref, mine_ref, other_ref, one_ref, two_ref):
    first = scal_ref[2] == 0
    down = lax.broadcasted_iota(jnp.int32, (CH, CH), 0)
    across = lax.broadcasted_iota(jnp.int32, (CH, CH), 1)
    eye = jnp.where(down == across, SCALE, 0.0).astype(BF16)
    for k in range(18):
        mine = mine_ref[:, k * CH : (k + 1) * CH]
        other = other_ref[:, k * CH : (k + 1) * CH]
        low, high = jnp.where(first, mine, other), jnp.where(first, other, mine)
        kernel = dot(eye, jnp.concatenate([low, high], axis=0), ((1,), (1,)))
        out_ref, at = (one_ref, k) if k < 9 else (two_ref, k - 9)
        out_ref[at * CH : (at + 1) * CH, :] = kernel


VM = pl.BlockSpec(memory_space=pltpu.VMEM)
SM = pl.BlockSpec(memory_space=pltpu.SMEM)
HB = pl.BlockSpec(memory_space=pltpu.HBM)


def call(body, outs, scratch, *args, flops=10**7, scalars=True, far_args=(), far_outs=()):
    moved = sum(math.prod(a.shape) * a.dtype.itemsize for a in args)
    moved += sum(math.prod(s) * jnp.dtype(t).itemsize for s, t in outs)
    args = [pltpu.with_memory_space_constraint(a, pltpu.HBM) if k in far_args else a for k, a in enumerate(args)]
    return pl.pallas_call(
        body,
        cost_estimate=pl.CostEstimate(flops=flops, bytes_accessed=moved, transcendentals=0),
        out_shape=[pltpu.HBM(s, t) if k in far_outs else jax.ShapeDtypeStruct(s, t) for k, (s, t) in enumerate(outs)],
        in_specs=[SM if scalars and k == 0 else HB if k in far_args else VM for k in range(len(args))],
        out_specs=[HB if k in far_outs else VM for k in range(len(outs))],
        scratch_shapes=scratch,
        compiler_params=pltpu.CompilerParams(vmem_limit_bytes=24 << 20),
    )(*args)


def block(
    field, weight_one, bias_one, weight_two, bias_two, depth_levels, fold_partner, cotangent
):
    n_low = lax.axis_size("z")
    n_high = lax.axis_size("yl") * lax.axis_size("x")
    n_z, n_m = n_low * n_high, 4
    merid = lax.axis_index(MERID)
    core = lax.axis_index("c")
    flat_field = field.reshape(ROWS * COLS, CH)
    flat_cot = cotangent.reshape(ROWS * COLS, CH)
    edge, rim = ((2 * ROWS, LANES), BF16), ((2 * COLS, LANES), BF16)
    flat_deep, top_rows, low_rows, west_edge, east_edge, far_edge = call(
        pack_kernel,
        [((ROWS * COLS, 128), BF16), rim, rim, edge, edge, ((4, LANES), BF16)],
        [
            pltpu.VMEM((2 * ROWS, LANES), F32),
            pltpu.VMEM((ROWS * COLS, CH), BF16),
            pltpu.VMEM((ROWS * COLS, CH), BF16),
            pltpu.VMEM((ROWS, COLS), jnp.int32),
            pltpu.SemaphoreType.DMA((3,)),
        ],
        flat_field, flat_cot, depth_levels, scalars=False, far_args=(0, 1, 2),
    )

    fold_partner, west_edge = lax.optimization_barrier((fold_partner, west_edge))
    shift = (fold_partner[0] + 1) % (n_z * COLS)
    quotient, rest = shift // COLS, shift % COLS
    scal = jnp.stack([(merid == n_m - 1).astype(jnp.int32), rest.astype(jnp.int32), core.astype(jnp.int32)])

    def hop(rows, target):
        route = [(m * n_m + n_m - 1, (target(m) % n_z) * n_m + n_m - 1) for m in range(n_z)]
        return lax.ppermute(rows, ZONAL + MERID, route)

    near = hop(top_rows, lambda m: m - 1)
    far = hop(far_edge, lambda m: m - 2)
    west = lax.ppermute(east_edge, ZONAL, [(i, (i + 1) % n_z) for i in range(n_z)])
    east = lax.ppermute(west_edge, ZONAL, [((i + 1) % n_z, i) for i in range(n_z)])
    strip = ((2 * PITCH, LANES), BF16)
    upper, lower, fold = call(
        strip_kernel,
        [strip, strip, ((2 * PITCH, 2 * CH), BF16)],
        [
            pltpu.VMEM((2 * ROWS, LANES), F32),
            pltpu.VMEM((2 * ROWS, LANES), F32),
            pltpu.VMEM((4, LANES), F32),
            pltpu.VMEM((16, LANES), F32),
            pltpu.VMEM((2 * PITCH, LANES), F32),
        ],
        scal, top_rows, low_rows, west, east, near, far,
    )

    def turn(rows, high):
        return hop(rows, lambda m: n_low * ((n_high - 1 - m // n_low + high) % n_high) + m % n_low)

    def slide(rows, low):
        return hop(rows, lambda m: n_low * (m // n_low) + n_low - 1 + low - m % n_low)

    fold = lax.switch(quotient // n_low, [lambda rows, h=h: turn(rows, h) for h in range(n_high)], fold)
    upper, lower, fold = lax.optimization_barrier((upper, lower, fold))
    south = lax.ppermute(upper, MERID, [(i, i + 1) for i in range(n_m - 1)])
    north = lax.ppermute(lower, MERID, [(i + 1, i) for i in range(n_m - 1)])
    fold = lax.switch(quotient % n_low, [lambda rows, h=h: slide(rows, h) for h in range(n_low)], fold)
    w1 = weight_one.reshape(9, CH, CH)
    w2 = weight_two.reshape(9, CH, CH)
    half = ((CH // 2, 9 * CH), F32)
    pf, pd, ph, slope, keep_two, send_two = call(
        first_kernel,
        [((EXT, 3 * CH), BF16), ((EXT, 3 * CH), BF16), ((MID, 3 * CH), BF16), ((MID, CH), F32), half, half],
        [
            pltpu.VMEM((EXT + 16, CH), F32),
            pltpu.VMEM((EXT, 128), F32),
            pltpu.VMEM((32, LANES), F32),
            pltpu.VMEM((32, LANES), F32),
            pltpu.VMEM((2 * PITCH, LANES), F32),
            pltpu.VMEM((2 * PITCH, LANES), F32),
            pltpu.VMEM((CH, INNER), BF16),
            pltpu.VMEM((9, CH, CH), BF16),
            pltpu.VMEM((MID, 3 * CH), BF16),
            pltpu.SemaphoreType.DMA((2,)),
        ],
        scal, flat_field, flat_cot, flat_deep, west, east, south, north, fold, w1, bias_one.reshape(1, CH),
        flops=3 * 10**9, far_args=(9,), far_outs=(2,),
    )
    swap = [(0, 1), (1, 0)]
    came_two = lax.ppermute(send_two, "c", swap)
    pe, keep_one, send_one = call(
        second_kernel,
        [((MID, 3 * CH), BF16), half, half],
        [
            pltpu.VMEM((MID + 16, CH), F32),
            pltpu.VMEM((CH, INNER), BF16),
            pltpu.VMEM((MID, 3 * CH), BF16),
            pltpu.SemaphoreType.DMA,
        ],
        scal, pd, pf, slope, w2,
        flops=3 * 10**9, far_outs=(0,),
    )
    came_one = lax.ppermute(send_one, "c", swap)
    output, input_grad = call(
        third_kernel,
        [((ROWS * COLS, CH), BF16), ((ROWS * COLS, CH), BF16)],
        [],
        scal, ph, pe, flat_field, flat_cot, flat_deep, w1, w2, bias_two.reshape(1, CH),
        flops=3 * 10**9,
    )

    n_p = lax.axis_size("yl") * lax.axis_size("x") * lax.axis_size("yh")
    rows = CH // 2 // n_p
    width = 18 * CH
    sums = jnp.concatenate([keep_one + came_one, keep_two + came_two], axis=1).astype(BF16)
    sums = lax.all_to_all(sums.reshape(n_p, rows, width), PLANE, 0, 0)
    sums = jnp.sum(sums.astype(F32), axis=0)
    part = rows // n_low
    sums = lax.all_to_all(sums.reshape(n_low, part * 36, 128), "z", 0, 0)
    piece = jnp.sum(sums, axis=0).astype(BF16)
    line = lax.all_to_all(jnp.broadcast_to(piece[None], (n_low, part * 36, 128)), "z", 0, 0)
    line = line.reshape(rows, width)
    mine = lax.all_to_all(jnp.broadcast_to(line[None], (n_p, rows, width)), PLANE, 0, 0)
    mine = mine.reshape(CH // 2, width)
    other = lax.ppermute(mine, "c", swap)
    grad_one, grad_two = call(
        last_kernel,
        [((9 * CH, CH), F32), ((9 * CH, CH), F32)],
        [],
        scal, mine, other,
    )
    return (
        output.reshape(ROWS, COLS, CH),
        input_grad.reshape(ROWS, COLS, CH),
        grad_one.reshape(3, 3, CH, CH),
        grad_two.reshape(3, 3, CH, CH),
    )


def solution(mesh):
    fine = Mesh(mesh.devices.reshape(SPLIT + (2, 2)), ZONAL + MERID)
    cells = P(MERID, ZONAL, None)
    return jax.shard_map(
        block,
        mesh=fine,
        in_specs=(cells, P(), P(), P(), P(), P(MERID, ZONAL), P(), cells),
        out_specs=(cells, cells, P(), P()),
        check_vma=False,
    )
```

```python
import math

import jax
import jax.numpy as jnp
from jax import lax
from jax.experimental import pallas as pl
from jax.experimental.pallas import tpu as pltpu
from jax.sharding import Mesh
from jax.sharding import PartitionSpec as P


LEV = 64
SPLIT = (2, 4, 8)
ZONAL = ("yl", "x", "z")
MERID = ("yh", "c")
PLANE = ("yl", "x", "yh")
SCALE = 1.0 / 512.0
ROWS = 16
COLS = 64
CH = 256
PITCH = 72
EXT = 20 * PITCH + 16
MID = 18 * PITCH + 8
INNER = 16 * PITCH
LANES = 2 * CH + 128
HEAD = 8
F32 = jnp.float32
BF16 = jnp.bfloat16
C0 = math.sqrt(2.0 / math.pi)
C1 = 0.044715


def dot(a, b, dims=((1,), (0,))):
    return lax.dot_general(a, b, (dims, ((), ())), preferred_element_type=F32)


def taps(lhs_ref, row, count, w_ref, picks, transposed):
    total = None
    for a, indices in picks:
        lhs = lhs_ref[row + a * PITCH : row + a * PITCH + count, :]
        side = jnp.concatenate([w_ref[k] for k in indices], axis=1 if transposed else 0)
        part = dot(lhs, side, ((1,), (1 if transposed else 0,)))
        total = part if total is None else total + part
    return total


def plain(rows_of=(0, 1, 2)):
    return [(a, [3 * a + b for b in range(3)]) for a in rows_of]


def turned(rows_of=(0, 1, 2)):
    return [(a, [8 - 3 * a - b for b in range(3)]) for a in rows_of]


def shifted(out_ref, src_ref, count):
    step = 112
    for start in range(0, count, step):
        size = min(step, count - start)
        for b in range(3):
            at = HEAD + start + b - 1
            out_ref[start : start + size, b * CH : (b + 1) * CH] = src_ref[at : at + size, :].astype(BF16)


def own_cells(count, first):
    place = (lax.broadcasted_iota(jnp.int32, (count, CH), 0) + first) % PITCH
    return place >= 8


def transposed_own(ref, first, out_ref):
    eye = (
        lax.broadcasted_iota(jnp.int32, (CH, CH), 0) == lax.broadcasted_iota(jnp.int32, (CH, CH), 1)
    ).astype(BF16)
    step = 128
    for start in range(0, INNER, step):
        cells = ref[first + start : first + start + step, CH : 2 * CH].astype(F32)
        cells = jnp.where(own_cells(step, start), cells, 0.0).astype(BF16)
        out_ref[:, start : start + step] = dot(eye, cells, ((1,), (1,))).astype(BF16)


def weight_grad(keep_ref, send_ref, core, turned_ref, patches_ref, row):
    for a in range(3):
        for b in range(3):
            cells = patches_ref[row + a * PITCH : row + a * PITCH + INNER, b * CH : (b + 1) * CH]
            at = (3 * a + b) * CH
            sums = dot(turned_ref[...], cells)
            low, high = sums[: CH // 2], sums[CH // 2 :]
            keep_ref[:, at : at + CH] = jnp.where(core == 0, low, high)
            send_ref[:, at : at + CH] = jnp.where(core == 0, high, low)


def pack_kernel(
    field_far, cot_far, dep_far, deep_ref, top_ref, low_ref, west_ref, east_ref,
    edge, field_ref, cot_ref, dep_ref, sems,
):
    copies = [
        pltpu.make_async_copy(dep_far, dep_ref, sems.at[0]),
        pltpu.make_async_copy(field_far, field_ref, sems.at[1]),
        pltpu.make_async_copy(cot_far, cot_ref, sems.at[2]),
    ]
    for copy in copies:
        copy.start()
    copies[0].wait()
    eye = (
        lax.broadcasted_iota(jnp.int32, (COLS, COLS), 0) == lax.broadcasted_iota(jnp.int32, (COLS, COLS), 1)
    ).astype(F32)
    ones = jnp.ones((COLS, 128), BF16)
    level = (lax.broadcasted_iota(jnp.int32, (1, CH), 1) % LEV).astype(F32)

    def masked(at, count):
        deep = deep_ref[at : at + count, :].astype(F32)
        keep = level < jnp.concatenate([deep, deep], axis=1)
        return jnp.where(keep, cot_ref[at : at + count, :].astype(F32), 0.0)

    for y in range(ROWS):
        line = dep_ref[y : y + 1, :].astype(F32)
        deep_ref[y * COLS : (y + 1) * COLS, :] = dot((eye * line).astype(BF16), ones).astype(BF16)
    copies[1].wait()
    copies[2].wait()
    for out_ref, first in ((top_ref, ROWS - 2), (low_ref, 0)):
        at = first * COLS
        out_ref[:, 0:CH] = field_ref[at : at + 2 * COLS, :]
        out_ref[:, CH : 2 * CH] = masked(at, 2 * COLS).astype(BF16)
        out_ref[:, 2 * CH : LANES] = deep_ref[at : at + 2 * COLS, :]
    for out_ref, column, skip in ((west_ref, 0, 0), (east_ref, COLS - 16, 14)):
        for y in range(ROWS):
            at = y * COLS + column
            cells = slice(2 * y, 2 * y + 2)
            edge[cells, 0:CH] = field_ref[at : at + 16, :].astype(F32)[skip : skip + 2]
            edge[cells, CH : 2 * CH] = masked(at, 16)[skip : skip + 2]
            edge[cells, 2 * CH : LANES] = deep_ref[at : at + 16, :].astype(F32)[skip : skip + 2]
        if skip:
            edge[2 * ROWS : 2 * ROWS + 8, :] = jnp.zeros((8, LANES), F32)
            for k in range(2):
                at = (ROWS - 2 + k) * COLS + column
                cells = slice(2 * ROWS + k, 2 * ROWS + k + 1)
                edge[cells, 0:CH] = field_ref[at : at + 16, :].astype(F32)[skip - 1 : skip]
                edge[cells, CH : 2 * CH] = masked(at, 16)[skip - 1 : skip]
                edge[cells, 2 * CH : LANES] = deep_ref[at : at + 16, :].astype(F32)[skip - 1 : skip]
        out_ref[...] = edge[0 : out_ref.shape[0], :].astype(BF16)


def strip_kernel(
    scal_ref, top_ref, low_ref, west_ref, east_ref, near_ref, upper_ref, lower_ref, fold_ref, west, east, extra, strip,
):
    west[...] = west_ref[...].astype(F32)
    east[...] = east_ref[...].astype(F32)
    strip[...] = jnp.zeros(strip.shape, F32)
    for out_ref, rows_ref, first in ((upper_ref, top_ref, ROWS - 2), (lower_ref, low_ref, 0)):
        for k in range(2):
            y, at = first + k, k * PITCH
            strip[at : at + COLS, :] = rows_ref[k * COLS : (k + 1) * COLS, :].astype(F32)
            strip[at + 64 : at + 66, :] = east[2 * y : 2 * y + 2, :]
            strip[at + 70 : at + 72, :] = west[2 * y : 2 * y + 2, :]
        out_ref[...] = strip[...].astype(BF16)
    to = lax.broadcasted_iota(jnp.int32, (PITCH, 144), 0)
    at = lax.broadcasted_iota(jnp.int32, (PITCH, 144), 1)
    want = 63 - jnp.where(to >= 70, to - PITCH, to) + scal_ref[1]
    want = jnp.where((to >= 66) & (to < 70), -98, want)
    have = jnp.where(at < 128, at, jnp.where(at < 130, at - 130, jnp.where(at == 130, -3, -99)))
    pick = (want == have).astype(F32).astype(BF16)
    extra[...] = jnp.zeros(extra.shape, F32)
    here = lax.broadcasted_iota(jnp.int32, (PITCH, 128), 0) == lax.broadcasted_iota(jnp.int32, (PITCH, 128), 1)
    third = lax.broadcasted_iota(jnp.int32, (8, 128), 0) == 2
    for j in range(2):
        i = 1 - j
        y = ROWS - 2 + i
        extra[0:2, :] = west[2 * y : 2 * y + 2, :]
        extra[2:3, :] = west[2 * ROWS + i : 2 * ROWS + i + 1, :]
        rows = slice(i * COLS, (i + 1) * COLS)
        cells = jnp.concatenate([top_ref[rows, :], near_ref[rows, :], extra[...].astype(BF16)], axis=0)
        cells = dot(pick, cells)
        fold_ref[j * PITCH : (j + 1) * PITCH, :] = cells[:, : 2 * CH].astype(BF16)
        line = jnp.sum(jnp.where(here, cells[:, 2 * CH :], 0.0), axis=0, keepdims=True)
        free = slice(j * PITCH + COLS, j * PITCH + COLS + 8)
        tile = jnp.where(third, jnp.broadcast_to(line, (8, 128)), cells[COLS:, :128])
        fold_ref[free, 0:128] = tile.astype(BF16)


def first_kernel(
    scal_ref, field_ref, cot_ref, dep_ref, west_ref, east_ref, south_ref, north_ref, fold_ref,
    w_far, bias_ref,
    pf_ref, pd_ref, ph_far, slope_ref, keep_ref, send_ref,
    ext, depth, west, east, south, north, back, w_ref, ph_ref, sems,
):
    weights = pltpu.make_async_copy(w_far, w_ref, sems.at[0])
    weights.start()
    top = scal_ref[0] == 1
    west[...] = west_ref[0 : 2 * ROWS, :].astype(F32)
    east[...] = east_ref[...].astype(F32)
    south[...] = south_ref[...].astype(F32)
    north[:, 0 : 2 * CH] = north_ref[:, 0 : 2 * CH].astype(F32) + fold_ref[...].astype(F32)
    here = lax.broadcasted_iota(jnp.int32, (PITCH, 128), 0) == lax.broadcasted_iota(jnp.int32, (PITCH, 128), 1)
    for j in range(2):
        tile = fold_ref[j * PITCH + COLS : j * PITCH + COLS + 8, 0:128].astype(F32)
        spread = jnp.where(here, jnp.broadcast_to(tile[2:3, :], (PITCH, 128)), 0.0).astype(BF16)
        rows = slice(j * PITCH, (j + 1) * PITCH)
        north[rows, 2 * CH :] = north_ref[rows, 2 * CH :].astype(F32) + dot(spread, jnp.ones((128, 128), BF16))

    def fill(out_ref, lanes, own, width, head):
        if head:
            out_ref[0:head, :] = jnp.zeros((head, width), F32)
        for g in range(21):
            base = head + g * PITCH
            out_ref[base : base + 8, :] = jnp.zeros((8, width), F32)
            y = g - 3
            if 0 <= y < 16:
                out_ref[base : base + 2, :] = east[2 * y : 2 * y + 2, lanes]
            elif -2 <= y < 0:
                at = (y + 2) * PITCH + 64
                out_ref[base : base + 2, :] = south[at : at + 2, lanes]
            elif y >= 16:
                at = (y - 16) * PITCH + 64
                out_ref[base : base + 2, :] = north[at : at + 2, lanes]
            y = g - 2
            if 0 <= y < 16:
                out_ref[base + 6 : base + 8, :] = west[2 * y : 2 * y + 2, lanes]
            elif -2 <= y < 0:
                at = (y + 2) * PITCH + 70
                out_ref[base + 6 : base + 8, :] = south[at : at + 2, lanes]
            elif 16 <= y < 18:
                at = (y - 16) * PITCH + 70
                out_ref[base + 6 : base + 8, :] = north[at : at + 2, lanes]
        for y in range(-2, 18):
            base = head + (y + 2) * PITCH + 8
            if y < 0:
                out_ref[base : base + 64, :] = south[(y + 2) * PITCH : (y + 2) * PITCH + 64, lanes]
            elif y < 16:
                out_ref[base : base + 64, :] = own(y)
            else:
                out_ref[base : base + 64, :] = north[(y - 16) * PITCH : (y - 16) * PITCH + 64, lanes]
        tail = head + 20 * PITCH + 8
        rest = out_ref.shape[0] - tail
        if rest:
            out_ref[tail:, :] = jnp.zeros((rest, width), F32)

    level = lax.broadcasted_iota(jnp.int32, (1, CH), 1) % LEV
    level = level.astype(F32)

    def wet(values):
        return level < jnp.concatenate([values, values], axis=1)

    def own_field(y):
        return field_ref[y * 64 : (y + 1) * 64, :].astype(F32)

    def own_depth(y):
        return dep_ref[y * 64 : (y + 1) * 64, :].astype(F32)

    def own_delta(y):
        cells = cot_ref[y * 64 : (y + 1) * 64, :].astype(F32)
        return jnp.where(wet(own_depth(y)), cells, 0.0)

    fill(ext, slice(0, CH), own_field, CH, HEAD)
    fill(depth, slice(2 * CH, LANES), own_depth, 128, 0)
    shifted(pf_ref, ext, EXT)
    fill(ext, slice(CH, 2 * CH), own_delta, CH, HEAD)
    shifted(pd_ref, ext, EXT)

    bias = bias_ref[...]
    weights.wait()

    def finish(pre, p):
        count = pre.shape[0]
        x = pre + bias
        square = x * x
        t = jnp.tanh(C0 * (x + C1 * (square * x)))
        keep = wet(depth[p : p + count, :])
        half = 0.5 * (1.0 + t)
        hidden = jnp.where(keep, x * half, 0.0).astype(BF16).astype(F32)
        slope = half + (0.5 * C0) * x * (1.0 - t * t) * (1.0 + (3.0 * C1) * square)
        return hidden, jnp.where(keep, slope, 0.0)

    first = 72
    step = 176
    for start in range(first, first + 1232, step):
        hidden, slope = finish(taps(pf_ref, start - PITCH, step, w_ref, plain(), False), start)
        ext[HEAD + start - first : HEAD + start - first + step, :] = hidden
        slope_ref[start - first : start - first + step, :] = slope
    start = 1296
    picks = [(a, [jnp.where(top, 8 - 3 * a - b, 3 * a + b) for b in range(3)]) for a in range(3)]
    hidden, slope = finish(taps(pf_ref, start - PITCH, 80, w_ref, picks, False), start)
    at = start - first
    beyond = lax.broadcasted_iota(jnp.int32, (8, CH), 0) >= 4
    ext[HEAD + at : HEAD + at + 8, :] = jnp.where(beyond, hidden[:8], ext[HEAD + at : HEAD + at + 8, :])
    slope_ref[at : at + 8, :] = jnp.where(beyond, slope[:8], slope_ref[at : at + 8, :])
    ext[HEAD + at + 8 : HEAD + at + 80, :] = hidden[8:]
    slope_ref[at + 8 : at + 80, :] = slope[8:]
    ext[HEAD + MID : HEAD + MID + 8, :] = jnp.zeros((8, CH), F32)
    shifted(ph_ref, ext, MID)
    leave = pltpu.make_async_copy(ph_ref, ph_far, sems.at[1])
    leave.start()
    transposed_own(pd_ref, 144, back)
    weight_grad(keep_ref, send_ref, scal_ref[2], back, ph_ref, 0)
    leave.wait()


def second_kernel(
    scal_ref, pd_ref, pf_ref, slope_ref, w_ref, pe_far, keep_ref, send_ref, ext, back, pe_ref, sem
):
    top = scal_ref[0] == 1
    first = 72
    ext[0:HEAD, :] = jnp.zeros((HEAD, CH), F32)
    ext[HEAD + MID : HEAD + MID + 8, :] = jnp.zeros((8, CH), F32)

    def put(sums, p):
        at = p - first
        count = sums.shape[0]
        delta = (slope_ref[at : at + count, :] * sums).astype(BF16).astype(F32)
        ext[HEAD + at : HEAD + at + count, :] = delta

    step = 232
    for start in range(first, first + 1160, step):
        put(taps(pd_ref, start - PITCH, step, w_ref, turned(), True), start)
    start = 1232
    sums = taps(pd_ref, start - PITCH, 144, w_ref, turned((0,)), True)
    over = [(2, [jnp.where(top, 6 + b, 2 - b) for b in range(3)])]
    sums = sums + taps(pd_ref, start - PITCH, 144, w_ref, over, True)
    middle = taps(pd_ref, start - PITCH, 72, w_ref, turned((1,)), True)
    beside = [(1, [jnp.where(top, 3 + b, 5 - b) for b in range(3)])]
    upper = taps(pd_ref, 1296 - PITCH, 80, w_ref, beside, True)
    beyond = lax.broadcasted_iota(jnp.int32, (8, CH), 0) >= 4
    put(sums[:64] + middle[:64], 1232)
    put(sums[64:72] + jnp.where(beyond, upper[:8], middle[64:]), 1296)
    put(sums[72:] + upper[8:], 1304)
    start = 1224
    gap = taps(pd_ref, start - PITCH, 16, w_ref, turned((0, 1)), True)
    gap = gap + taps(pd_ref, start - PITCH, 16, w_ref, over, True)
    at = start - first
    delta = (slope_ref[at : at + 8, :] * gap[:8]).astype(BF16).astype(F32)
    ext[HEAD + at : HEAD + at + 8, :] = jnp.where(beyond, delta, ext[HEAD + at : HEAD + at + 8, :])
    shifted(pe_ref, ext, MID)
    leave = pltpu.make_async_copy(pe_ref, pe_far, sem)
    leave.start()
    transposed_own(pe_ref, 72, back)
    weight_grad(keep_ref, send_ref, scal_ref[2], back, pf_ref, 72)
    leave.wait()


def third_kernel(
    scal_ref, ph_ref, pe_ref, field_ref, cot_ref, dep_ref, w1_ref, w2_ref, bias_ref, out_ref, in_ref
):
    top = scal_ref[0] == 1
    level = (lax.broadcasted_iota(jnp.int32, (1, CH), 1) % LEV).astype(F32)
    bias = bias_ref[...]

    def wet(at):
        deep = dep_ref[at, :].astype(F32)
        return level < jnp.concatenate([deep, deep], axis=1)

    for y in range(0, 16, 4):
        p = 144 + y * PITCH
        sums = taps(ph_ref, p - 144, 4 * PITCH, w2_ref, plain(), False)
        for k in range(4):
            at = slice((y + k) * 64, (y + k + 1) * 64)
            cells = field_ref[at, :].astype(F32) + sums[k * PITCH + 8 : (k + 1) * PITCH] + bias
            out_ref[at, :] = jnp.where(wet(at), cells, 0.0).astype(BF16)

    def put(cells, y):
        at = slice(y * 64, (y + 1) * 64)
        total = jnp.where(wet(at), cot_ref[at, :].astype(F32), 0.0) + cells
        in_ref[at, :] = total.astype(BF16)

    for y in range(0, 15, 5):
        p = 144 + y * PITCH
        sums = taps(pe_ref, p - 144, 5 * PITCH, w1_ref, turned(), True)
        for k in range(5):
            put(sums[k * PITCH + 8 : (k + 1) * PITCH], y + k)
    p = 144 + 15 * PITCH + 8
    over = [(2, [jnp.where(top, 6 + b, 2 - b) for b in range(3)])]
    sums = taps(pe_ref, p - 144, 64, w1_ref, turned((0, 1)), True)
    put(sums + taps(pe_ref, p - 144, 64, w1_ref, over, True), 15)


def join_kernel(keep_one, came_one, keep_two, came_two, out_ref):
    width = 9 * CH
    for at in range(0, CH // 2, 16):
        rows = slice(at, at + 16)
        out_ref[rows, 0:width] = (keep_one[rows, :] + came_one[rows, :]).astype(BF16)
        out_ref[rows, width:] = (keep_two[rows, :] + came_two[rows, :]).astype(BF16)


def total_kernel(parts_ref, out_ref):
    count, _, width = parts_ref.shape
    step = 512
    for at in range(0, width, step):
        total = parts_ref[0, :, at : at + step].astype(F32)
        for k in range(1, count):
            total = total + parts_ref[k, :, at : at + step].astype(F32)
        out_ref[:, at : at + step] = total


def last_kernel(scal_ref, mine_ref, other_ref, one_ref, two_ref):
    first = scal_ref[2] == 0
    down = lax.broadcasted_iota(jnp.int32, (CH, CH), 0)
    across = lax.broadcasted_iota(jnp.int32, (CH, CH), 1)
    eye = jnp.where(down == across, SCALE, 0.0).astype(BF16)
    for k in range(18):
        mine = mine_ref[:, k * CH : (k + 1) * CH]
        other = other_ref[:, k * CH : (k + 1) * CH]
        low, high = jnp.where(first, mine, other), jnp.where(first, other, mine)
        kernel = dot(eye, jnp.concatenate([low, high], axis=0), ((1,), (1,)))
        out_ref, at = (one_ref, k) if k < 9 else (two_ref, k - 9)
        out_ref[at * CH : (at + 1) * CH, :] = kernel


VM = pl.BlockSpec(memory_space=pltpu.VMEM)
SM = pl.BlockSpec(memory_space=pltpu.SMEM)
HB = pl.BlockSpec(memory_space=pltpu.HBM)


def call(body, outs, scratch, *args, flops=10**7, scalars=True, far_args=(), far_outs=()):
    moved = sum(math.prod(a.shape) * a.dtype.itemsize for a in args)
    moved += sum(math.prod(s) * jnp.dtype(t).itemsize for s, t in outs)
    args = [pltpu.with_memory_space_constraint(a, pltpu.HBM) if k in far_args else a for k, a in enumerate(args)]
    return pl.pallas_call(
        body,
        cost_estimate=pl.CostEstimate(flops=flops, bytes_accessed=moved, transcendentals=0),
        out_shape=[pltpu.HBM(s, t) if k in far_outs else jax.ShapeDtypeStruct(s, t) for k, (s, t) in enumerate(outs)],
        in_specs=[SM if scalars and k == 0 else HB if k in far_args else VM for k in range(len(args))],
        out_specs=[HB if k in far_outs else VM for k in range(len(outs))],
        scratch_shapes=scratch,
        compiler_params=pltpu.CompilerParams(vmem_limit_bytes=24 << 20),
    )(*args)


def block(
    field, weight_one, bias_one, weight_two, bias_two, depth_levels, fold_partner, cotangent
):
    n_low = lax.axis_size("z")
    n_high = lax.axis_size("yl") * lax.axis_size("x")
    n_z, n_m = n_low * n_high, 4
    merid = lax.axis_index(MERID)
    core = lax.axis_index("c")
    flat_field = field.reshape(ROWS * COLS, CH)
    flat_cot = cotangent.reshape(ROWS * COLS, CH)
    edge, rim = ((2 * ROWS, LANES), BF16), ((2 * COLS, LANES), BF16)
    flat_deep, top_rows, low_rows, west_edge, east_edge = call(
        pack_kernel,
        [((ROWS * COLS, 128), BF16), rim, rim, edge, ((2 * ROWS + 8, LANES), BF16)],
        [
            pltpu.VMEM((2 * ROWS + 8, LANES), F32),
            pltpu.VMEM((ROWS * COLS, CH), BF16),
            pltpu.VMEM((ROWS * COLS, CH), BF16),
            pltpu.VMEM((ROWS, COLS), jnp.int32),
            pltpu.SemaphoreType.DMA((3,)),
        ],
        flat_field, flat_cot, depth_levels, scalars=False, far_args=(0, 1, 2),
    )

    fold_partner, west_edge = lax.optimization_barrier((fold_partner, west_edge))
    shift = fold_partner[0] + 2
    quotient, rest = shift // COLS % n_z, shift % COLS - 1
    scal = jnp.stack([(merid == n_m - 1).astype(jnp.int32), rest.astype(jnp.int32), core.astype(jnp.int32)])

    def hop(rows, target):
        route = [(m * n_m + n_m - 1, (target(m) % n_z) * n_m + n_m - 1) for m in range(n_z)]
        return lax.ppermute(rows, ZONAL + MERID, route)

    near = hop(top_rows, lambda m: m - 1)
    west = lax.ppermute(east_edge, ZONAL, [(i, (i + 1) % n_z) for i in range(n_z)])
    east = lax.ppermute(west_edge, ZONAL, [((i + 1) % n_z, i) for i in range(n_z)])
    strip = ((2 * PITCH, LANES), BF16)
    upper, lower, fold = call(
        strip_kernel,
        [strip, strip, ((2 * PITCH, 2 * CH), BF16)],
        [
            pltpu.VMEM((2 * ROWS + 8, LANES), F32),
            pltpu.VMEM((2 * ROWS, LANES), F32),
            pltpu.VMEM((16, LANES), F32),
            pltpu.VMEM((2 * PITCH, LANES), F32),
        ],
        scal, top_rows, low_rows, west, east, near,
    )

    def turn(rows, high):
        return hop(rows, lambda m: n_low * ((n_high - 1 - m // n_low + high) % n_high) + m % n_low)

    def slide(rows, low):
        return hop(rows, lambda m: n_low * (m // n_low) + n_low - 1 + low - m % n_low)

    fold = lax.switch(quotient // n_low, [lambda rows, h=h: turn(rows, h) for h in range(n_high)], fold)
    upper, lower, fold = lax.optimization_barrier((upper, lower, fold))
    south = lax.ppermute(upper, MERID, [(i, i + 1) for i in range(n_m - 1)])
    north = lax.ppermute(lower, MERID, [(i + 1, i) for i in range(n_m - 1)])
    fold = lax.switch(quotient % n_low, [lambda rows, h=h: slide(rows, h) for h in range(n_low)], fold)
    w1 = weight_one.reshape(9, CH, CH)
    w2 = weight_two.reshape(9, CH, CH)
    half = ((CH // 2, 9 * CH), F32)
    pf, pd, ph, slope, keep_two, send_two = call(
        first_kernel,
        [((EXT, 3 * CH), BF16), ((EXT, 3 * CH), BF16), ((MID, 3 * CH), BF16), ((MID, CH), F32), half, half],
        [
            pltpu.VMEM((EXT + 16, CH), F32),
            pltpu.VMEM((EXT, 128), F32),
            pltpu.VMEM((32, LANES), F32),
            pltpu.VMEM((32, LANES), F32),
            pltpu.VMEM((2 * PITCH, LANES), F32),
            pltpu.VMEM((2 * PITCH, LANES), F32),
            pltpu.VMEM((CH, INNER), BF16),
            pltpu.VMEM((9, CH, CH), BF16),
            pltpu.VMEM((MID, 3 * CH), BF16),
            pltpu.SemaphoreType.DMA((2,)),
        ],
        scal, flat_field, flat_cot, flat_deep, west, east, south, north, fold, w1, bias_one.reshape(1, CH),
        flops=3 * 10**9, far_args=(9,), far_outs=(2,),
    )
    swap = [(0, 1), (1, 0)]
    came_two = lax.ppermute(send_two, "c", swap)
    pe, keep_one, send_one = call(
        second_kernel,
        [((MID, 3 * CH), BF16), half, half],
        [
            pltpu.VMEM((MID + 16, CH), F32),
            pltpu.VMEM((CH, INNER), BF16),
            pltpu.VMEM((MID, 3 * CH), BF16),
            pltpu.SemaphoreType.DMA,
        ],
        scal, pd, pf, slope, w2,
        flops=3 * 10**9, far_outs=(0,),
    )
    came_one = lax.ppermute(send_one, "c", swap)
    output, input_grad = call(
        third_kernel,
        [((ROWS * COLS, CH), BF16), ((ROWS * COLS, CH), BF16)],
        [],
        scal, ph, pe, flat_field, flat_cot, flat_deep, w1, w2, bias_two.reshape(1, CH),
        flops=3 * 10**9,
    )

    n_p = lax.axis_size("yl") * lax.axis_size("x") * lax.axis_size("yh")
    rows = CH // 2 // n_p
    width = 18 * CH
    (sums,) = call(join_kernel, [((CH // 2, width), BF16)], [], keep_one, came_one, keep_two, came_two, scalars=False)
    sums = lax.all_to_all(sums.reshape(n_p, rows, width), PLANE, 0, 0)
    (sums,) = call(total_kernel, [((rows, width), F32)], [], sums, scalars=False)
    part = rows // n_low
    sums = lax.all_to_all(sums.reshape(n_low, part * 36, 128), "z", 0, 0)
    piece = jnp.sum(sums, axis=0).astype(BF16)
    line = lax.all_to_all(jnp.broadcast_to(piece[None], (n_low, part * 36, 128)), "z", 0, 0)
    line = line.reshape(rows, width)
    mine = lax.all_to_all(jnp.broadcast_to(line[None], (n_p, rows, width)), PLANE, 0, 0)
    mine = mine.reshape(CH // 2, width)
    other = lax.ppermute(mine, "c", swap)
    grad_one, grad_two = call(
        last_kernel,
        [((9 * CH, CH), F32), ((9 * CH, CH), F32)],
        [],
        scal, mine, other,
    )
    return (
        output.reshape(ROWS, COLS, CH),
        input_grad.reshape(ROWS, COLS, CH),
        grad_one.reshape(3, 3, CH, CH),
        grad_two.reshape(3, 3, CH, CH),
    )


def solution(mesh):
    fine = Mesh(mesh.devices.reshape(SPLIT + (2, 2)), ZONAL + MERID)
    cells = P(MERID, ZONAL, None)
    return jax.shard_map(
        block,
        mesh=fine,
        in_specs=(cells, P(), P(), P(), P(), P(MERID, ZONAL), P(), cells),
        out_specs=(cells, cells, P(), P()),
        check_vma=False,
    )
```

```python
import math

import jax
import jax.numpy as jnp
from jax import lax
from jax.experimental import pallas as pl
from jax.experimental.pallas import tpu as pltpu
from jax.sharding import Mesh
from jax.sharding import PartitionSpec as P


LEV = 64
SPLIT = (2, 4, 8)
ZONAL = ("yl", "x", "z")
MERID = ("yh", "c")
PLANE = ("yl", "x", "yh")
SCALE = 1.0 / 512.0
ROWS = 16
COLS = 64
CH = 256
PITCH = 72
EXT = 20 * PITCH + 16
MID = 18 * PITCH + 8
INNER = 16 * PITCH
LANES = 2 * CH + 128
HEAD = 8
F32 = jnp.float32
BF16 = jnp.bfloat16
C0 = math.sqrt(2.0 / math.pi)
C1 = 0.044715


def dot(a, b, dims=((1,), (0,))):
    return lax.dot_general(a, b, (dims, ((), ())), preferred_element_type=F32)


def taps(lhs_ref, row, count, w_ref, picks, transposed):
    total = None
    for a, indices in picks:
        lhs = lhs_ref[row + a * PITCH : row + a * PITCH + count, :]
        side = jnp.concatenate([w_ref[k] for k in indices], axis=1 if transposed else 0)
        part = dot(lhs, side, ((1,), (1 if transposed else 0,)))
        total = part if total is None else total + part
    return total


def plain(rows_of=(0, 1, 2)):
    return [(a, [3 * a + b for b in range(3)]) for a in rows_of]


def turned(rows_of=(0, 1, 2)):
    return [(a, [8 - 3 * a - b for b in range(3)]) for a in rows_of]


def shifted(out_ref, src_ref, count):
    step = 112
    for start in range(0, count, step):
        size = min(step, count - start)
        for b in range(3):
            at = HEAD + start + b - 1
            out_ref[start : start + size, b * CH : (b + 1) * CH] = src_ref[at : at + size, :].astype(BF16)


def own_cells(count, first):
    place = (lax.broadcasted_iota(jnp.int32, (count, CH), 0) + first) % PITCH
    return place >= 8


def transposed_own(ref, first, out_ref):
    eye = (
        lax.broadcasted_iota(jnp.int32, (CH, CH), 0) == lax.broadcasted_iota(jnp.int32, (CH, CH), 1)
    ).astype(BF16)
    step = 128
    for start in range(0, INNER, step):
        cells = ref[first + start : first + start + step, CH : 2 * CH].astype(F32)
        cells = jnp.where(own_cells(step, start), cells, 0.0).astype(BF16)
        out_ref[:, start : start + step] = dot(eye, cells, ((1,), (1,))).astype(BF16)


def weight_grad(keep_ref, send_ref, core, turned_ref, patches_ref, row):
    for a in range(3):
        for b in range(3):
            cells = patches_ref[row + a * PITCH : row + a * PITCH + INNER, b * CH : (b + 1) * CH]
            at = (3 * a + b) * CH
            sums = dot(turned_ref[...], cells)
            low, high = sums[: CH // 2], sums[CH // 2 :]
            keep_ref[:, at : at + CH] = jnp.where(core == 0, low, high)
            send_ref[:, at : at + CH] = jnp.where(core == 0, high, low)


def pack_kernel(
    field_far, cot_far, dep_far, deep_ref, top_ref, low_ref, west_ref, east_ref,
    edge, field_ref, cot_ref, dep_ref, sems,
):
    copies = [
        pltpu.make_async_copy(dep_far, dep_ref, sems.at[0]),
        pltpu.make_async_copy(field_far, field_ref, sems.at[1]),
        pltpu.make_async_copy(cot_far, cot_ref, sems.at[2]),
    ]
    for copy in copies:
        copy.start()
    copies[0].wait()
    eye = (
        lax.broadcasted_iota(jnp.int32, (COLS, COLS), 0) == lax.broadcasted_iota(jnp.int32, (COLS, COLS), 1)
    ).astype(F32)
    ones = jnp.ones((COLS, 128), BF16)
    level = (lax.broadcasted_iota(jnp.int32, (1, CH), 1) % LEV).astype(F32)

    def masked(at, count):
        deep = deep_ref[at : at + count, :].astype(F32)
        keep = level < jnp.concatenate([deep, deep], axis=1)
        return jnp.where(keep, cot_ref[at : at + count, :].astype(F32), 0.0)

    for y in range(ROWS):
        line = dep_ref[y : y + 1, :].astype(F32)
        deep_ref[y * COLS : (y + 1) * COLS, :] = dot((eye * line).astype(BF16), ones).astype(BF16)
    copies[1].wait()
    copies[2].wait()
    for out_ref, first in ((top_ref, ROWS - 2), (low_ref, 0)):
        at = first * COLS
        out_ref[:, 0:CH] = field_ref[at : at + 2 * COLS, :]
        out_ref[:, CH : 2 * CH] = masked(at, 2 * COLS).astype(BF16)
        out_ref[:, 2 * CH : LANES] = deep_ref[at : at + 2 * COLS, :]
    for out_ref, column, skip in ((west_ref, 0, 0), (east_ref, COLS - 16, 14)):
        for y in range(ROWS):
            at = y * COLS + column
            cells = slice(2 * y, 2 * y + 2)
            edge[cells, 0:CH] = field_ref[at : at + 16, :].astype(F32)[skip : skip + 2]
            edge[cells, CH : 2 * CH] = masked(at, 16)[skip : skip + 2]
            edge[cells, 2 * CH : LANES] = deep_ref[at : at + 16, :].astype(F32)[skip : skip + 2]
        if skip:
            edge[2 * ROWS : 2 * ROWS + 8, :] = jnp.zeros((8, LANES), F32)
            for k in range(2):
                at = (ROWS - 2 + k) * COLS + column
                cells = slice(2 * ROWS + k, 2 * ROWS + k + 1)
                edge[cells, 0:CH] = field_ref[at : at + 16, :].astype(F32)[skip - 1 : skip]
                edge[cells, CH : 2 * CH] = masked(at, 16)[skip - 1 : skip]
                edge[cells, 2 * CH : LANES] = deep_ref[at : at + 16, :].astype(F32)[skip - 1 : skip]
        out_ref[...] = edge[0 : out_ref.shape[0], :].astype(BF16)


def strip_kernel(
    scal_ref, top_ref, low_ref, west_ref, east_ref, near_ref, inner_ref, outer_ref, fold_ref, west, east, extra,
    upper, lower,
):
    west[...] = west_ref[...].astype(F32)
    east[...] = east_ref[...].astype(F32)
    for strip, rows_ref, first in ((upper, top_ref, ROWS - 2), (lower, low_ref, 0)):
        strip[...] = jnp.zeros(strip.shape, F32)
        for k in range(2):
            y, at = first + k, k * PITCH
            strip[at : at + COLS, :] = rows_ref[k * COLS : (k + 1) * COLS, :].astype(F32)
            strip[at + 64 : at + 66, :] = east[2 * y : 2 * y + 2, :]
            strip[at + 70 : at + 72, :] = west[2 * y : 2 * y + 2, :]
    first = scal_ref[2] == 0
    inner_ref[...] = jnp.where(first, upper[...], lower[...]).astype(BF16)
    outer_ref[...] = jnp.where(first, lower[...], upper[...]).astype(BF16)
    to = lax.broadcasted_iota(jnp.int32, (PITCH, 144), 0)
    at = lax.broadcasted_iota(jnp.int32, (PITCH, 144), 1)
    want = 63 - jnp.where(to >= 70, to - PITCH, to) + scal_ref[1]
    want = jnp.where((to >= 66) & (to < 70), -98, want)
    have = jnp.where(at < 128, at, jnp.where(at < 130, at - 130, jnp.where(at == 130, -3, -99)))
    pick = (want == have).astype(F32).astype(BF16)
    extra[...] = jnp.zeros(extra.shape, F32)
    here = lax.broadcasted_iota(jnp.int32, (PITCH, 128), 0) == lax.broadcasted_iota(jnp.int32, (PITCH, 128), 1)
    third = lax.broadcasted_iota(jnp.int32, (8, 128), 0) == 2
    for j in range(2):
        i = 1 - j
        y = ROWS - 2 + i
        extra[0:2, :] = west[2 * y : 2 * y + 2, :]
        extra[2:3, :] = west[2 * ROWS + i : 2 * ROWS + i + 1, :]
        rows = slice(i * COLS, (i + 1) * COLS)
        cells = jnp.concatenate([top_ref[rows, :], near_ref[rows, :], extra[...].astype(BF16)], axis=0)
        cells = dot(pick, cells)
        fold_ref[j * PITCH : (j + 1) * PITCH, :] = cells[:, : 2 * CH].astype(BF16)
        line = jnp.sum(jnp.where(here, cells[:, 2 * CH :], 0.0), axis=0, keepdims=True)
        free = slice(j * PITCH + COLS, j * PITCH + COLS + 8)
        tile = jnp.where(third, jnp.broadcast_to(line, (8, 128)), cells[COLS:, :128])
        fold_ref[free, 0:128] = tile.astype(BF16)


def first_kernel(
    scal_ref, field_ref, cot_ref, dep_ref, west_ref, east_ref, inner_ref, outer_ref, fold_ref,
    w_far, bias_ref,
    pf_ref, pd_ref, ph_far, slope_ref, keep_ref, send_ref,
    ext, depth, west, east, south, north, back, w_ref, ph_ref, sems,
):
    weights = pltpu.make_async_copy(w_far, w_ref, sems.at[0])
    weights.start()
    top = scal_ref[0] == 1
    west[...] = west_ref[0 : 2 * ROWS, :].astype(F32)
    east[...] = east_ref[...].astype(F32)
    core_first = scal_ref[2] == 0
    inner, outer = inner_ref[...].astype(F32), outer_ref[...].astype(F32)
    south[...] = jnp.where(core_first, outer, inner)
    north[...] = jnp.where(core_first, inner, outer)
    north[:, 0 : 2 * CH] = north[:, 0 : 2 * CH] + fold_ref[...].astype(F32)
    here = lax.broadcasted_iota(jnp.int32, (PITCH, 128), 0) == lax.broadcasted_iota(jnp.int32, (PITCH, 128), 1)
    for j in range(2):
        tile = fold_ref[j * PITCH + COLS : j * PITCH + COLS + 8, 0:128].astype(F32)
        spread = jnp.where(here, jnp.broadcast_to(tile[2:3, :], (PITCH, 128)), 0.0).astype(BF16)
        rows = slice(j * PITCH, (j + 1) * PITCH)
        north[rows, 2 * CH :] = north[rows, 2 * CH :] + dot(spread, jnp.ones((128, 128), BF16))

    def fill(out_ref, lanes, own, width, head):
        if head:
            out_ref[0:head, :] = jnp.zeros((head, width), F32)
        for g in range(21):
            base = head + g * PITCH
            out_ref[base : base + 8, :] = jnp.zeros((8, width), F32)
            y = g - 3
            if 0 <= y < 16:
                out_ref[base : base + 2, :] = east[2 * y : 2 * y + 2, lanes]
            elif -2 <= y < 0:
                at = (y + 2) * PITCH + 64
                out_ref[base : base + 2, :] = south[at : at + 2, lanes]
            elif y >= 16:
                at = (y - 16) * PITCH + 64
                out_ref[base : base + 2, :] = north[at : at + 2, lanes]
            y = g - 2
            if 0 <= y < 16:
                out_ref[base + 6 : base + 8, :] = west[2 * y : 2 * y + 2, lanes]
            elif -2 <= y < 0:
                at = (y + 2) * PITCH + 70
                out_ref[base + 6 : base + 8, :] = south[at : at + 2, lanes]
            elif 16 <= y < 18:
                at = (y - 16) * PITCH + 70
                out_ref[base + 6 : base + 8, :] = north[at : at + 2, lanes]
        for y in range(-2, 18):
            base = head + (y + 2) * PITCH + 8
            if y < 0:
                out_ref[base : base + 64, :] = south[(y + 2) * PITCH : (y + 2) * PITCH + 64, lanes]
            elif y < 16:
                out_ref[base : base + 64, :] = own(y)
            else:
                out_ref[base : base + 64, :] = north[(y - 16) * PITCH : (y - 16) * PITCH + 64, lanes]
        tail = head + 20 * PITCH + 8
        rest = out_ref.shape[0] - tail
        if rest:
            out_ref[tail:, :] = jnp.zeros((rest, width), F32)

    level = lax.broadcasted_iota(jnp.int32, (1, CH), 1) % LEV
    level = level.astype(F32)

    def wet(values):
        return level < jnp.concatenate([values, values], axis=1)

    def own_field(y):
        return field_ref[y * 64 : (y + 1) * 64, :].astype(F32)

    def own_depth(y):
        return dep_ref[y * 64 : (y + 1) * 64, :].astype(F32)

    def own_delta(y):
        cells = cot_ref[y * 64 : (y + 1) * 64, :].astype(F32)
        return jnp.where(wet(own_depth(y)), cells, 0.0)

    fill(ext, slice(0, CH), own_field, CH, HEAD)
    fill(depth, slice(2 * CH, LANES), own_depth, 128, 0)
    shifted(pf_ref, ext, EXT)
    fill(ext, slice(CH, 2 * CH), own_delta, CH, HEAD)
    shifted(pd_ref, ext, EXT)

    bias = bias_ref[...]
    weights.wait()

    def finish(pre, p):
        count = pre.shape[0]
        x = pre + bias
        square = x * x
        t = jnp.tanh(C0 * (x + C1 * (square * x)))
        keep = wet(depth[p : p + count, :])
        half = 0.5 * (1.0 + t)
        hidden = jnp.where(keep, x * half, 0.0).astype(BF16).astype(F32)
        slope = half + (0.5 * C0) * x * (1.0 - t * t) * (1.0 + (3.0 * C1) * square)
        return hidden, jnp.where(keep, slope, 0.0)

    first = 72
    step = 176
    for start in range(first, first + 1232, step):
        hidden, slope = finish(taps(pf_ref, start - PITCH, step, w_ref, plain(), False), start)
        ext[HEAD + start - first : HEAD + start - first + step, :] = hidden
        slope_ref[start - first : start - first + step, :] = slope
    start = 1296
    picks = [(a, [jnp.where(top, 8 - 3 * a - b, 3 * a + b) for b in range(3)]) for a in range(3)]
    hidden, slope = finish(taps(pf_ref, start - PITCH, 80, w_ref, picks, False), start)
    at = start - first
    beyond = lax.broadcasted_iota(jnp.int32, (8, CH), 0) >= 4
    ext[HEAD + at : HEAD + at + 8, :] = jnp.where(beyond, hidden[:8], ext[HEAD + at : HEAD + at + 8, :])
    slope_ref[at : at + 8, :] = jnp.where(beyond, slope[:8], slope_ref[at : at + 8, :])
    ext[HEAD + at + 8 : HEAD + at + 80, :] = hidden[8:]
    slope_ref[at + 8 : at + 80, :] = slope[8:]
    ext[HEAD + MID : HEAD + MID + 8, :] = jnp.zeros((8, CH), F32)
    shifted(ph_ref, ext, MID)
    leave = pltpu.make_async_copy(ph_ref, ph_far, sems.at[1])
    leave.start()
    transposed_own(pd_ref, 144, back)
    weight_grad(keep_ref, send_ref, scal_ref[2], back, ph_ref, 0)
    leave.wait()


def second_kernel(
    scal_ref, pd_ref, pf_ref, slope_ref, w_ref, pe_far, keep_ref, send_ref, ext, back, pe_ref, sem
):
    top = scal_ref[0] == 1
    first = 72
    ext[0:HEAD, :] = jnp.zeros((HEAD, CH), F32)
    ext[HEAD + MID : HEAD + MID + 8, :] = jnp.zeros((8, CH), F32)

    def put(sums, p):
        at = p - first
        count = sums.shape[0]
        delta = (slope_ref[at : at + count, :] * sums).astype(BF16).astype(F32)
        ext[HEAD + at : HEAD + at + count, :] = delta

    step = 232
    for start in range(first, first + 1160, step):
        put(taps(pd_ref, start - PITCH, step, w_ref, turned(), True), start)
    start = 1232
    sums = taps(pd_ref, start - PITCH, 144, w_ref, turned((0,)), True)
    over = [(2, [jnp.where(top, 6 + b, 2 - b) for b in range(3)])]
    sums = sums + taps(pd_ref, start - PITCH, 144, w_ref, over, True)
    middle = taps(pd_ref, start - PITCH, 72, w_ref, turned((1,)), True)
    beside = [(1, [jnp.where(top, 3 + b, 5 - b) for b in range(3)])]
    upper = taps(pd_ref, 1296 - PITCH, 80, w_ref, beside, True)
    beyond = lax.broadcasted_iota(jnp.int32, (8, CH), 0) >= 4
    put(sums[:64] + middle[:64], 1232)
    put(sums[64:72] + jnp.where(beyond, upper[:8], middle[64:]), 1296)
    put(sums[72:] + upper[8:], 1304)
    start = 1224
    gap = taps(pd_ref, start - PITCH, 16, w_ref, turned((0, 1)), True)
    gap = gap + taps(pd_ref, start - PITCH, 16, w_ref, over, True)
    at = start - first
    delta = (slope_ref[at : at + 8, :] * gap[:8]).astype(BF16).astype(F32)
    ext[HEAD + at : HEAD + at + 8, :] = jnp.where(beyond, delta, ext[HEAD + at : HEAD + at + 8, :])
    shifted(pe_ref, ext, MID)
    leave = pltpu.make_async_copy(pe_ref, pe_far, sem)
    leave.start()
    transposed_own(pe_ref, 72, back)
    weight_grad(keep_ref, send_ref, scal_ref[2], back, pf_ref, 72)
    leave.wait()


def third_kernel(
    scal_ref, ph_ref, pe_ref, field_ref, cot_ref, dep_ref, w1_ref, w2_ref, bias_ref, out_ref, in_ref
):
    top = scal_ref[0] == 1
    level = (lax.broadcasted_iota(jnp.int32, (1, CH), 1) % LEV).astype(F32)
    bias = bias_ref[...]

    def wet(at):
        deep = dep_ref[at, :].astype(F32)
        return level < jnp.concatenate([deep, deep], axis=1)

    for y in range(0, 16, 4):
        p = 144 + y * PITCH
        sums = taps(ph_ref, p - 144, 4 * PITCH, w2_ref, plain(), False)
        for k in range(4):
            at = slice((y + k) * 64, (y + k + 1) * 64)
            cells = field_ref[at, :].astype(F32) + sums[k * PITCH + 8 : (k + 1) * PITCH] + bias
            out_ref[at, :] = jnp.where(wet(at), cells, 0.0).astype(BF16)

    def put(cells, y):
        at = slice(y * 64, (y + 1) * 64)
        total = jnp.where(wet(at), cot_ref[at, :].astype(F32), 0.0) + cells
        in_ref[at, :] = total.astype(BF16)

    for y in range(0, 15, 5):
        p = 144 + y * PITCH
        sums = taps(pe_ref, p - 144, 5 * PITCH, w1_ref, turned(), True)
        for k in range(5):
            put(sums[k * PITCH + 8 : (k + 1) * PITCH], y + k)
    p = 144 + 15 * PITCH + 8
    over = [(2, [jnp.where(top, 6 + b, 2 - b) for b in range(3)])]
    sums = taps(pe_ref, p - 144, 64, w1_ref, turned((0, 1)), True)
    put(sums + taps(pe_ref, p - 144, 64, w1_ref, over, True), 15)


def join_kernel(keep_one, came_one, keep_two, came_two, out_ref):
    width = 9 * CH
    for at in range(0, CH // 2, 16):
        rows = slice(at, at + 16)
        out_ref[rows, 0:width] = (keep_one[rows, :] + came_one[rows, :]).astype(BF16)
        out_ref[rows, width:] = (keep_two[rows, :] + came_two[rows, :]).astype(BF16)


def total_kernel(parts_ref, out_ref):
    count, _, width = parts_ref.shape
    step = 512
    for at in range(0, width, step):
        total = parts_ref[0, :, at : at + step].astype(F32)
        for k in range(1, count):
            total = total + parts_ref[k, :, at : at + step].astype(F32)
        out_ref[:, at : at + step] = total


def last_kernel(scal_ref, mine_ref, other_ref, one_ref, two_ref):
    first = scal_ref[2] == 0
    down = lax.broadcasted_iota(jnp.int32, (CH, CH), 0)
    across = lax.broadcasted_iota(jnp.int32, (CH, CH), 1)
    eye = jnp.where(down == across, SCALE, 0.0).astype(BF16)
    for k in range(18):
        mine = mine_ref[:, k * CH : (k + 1) * CH]
        other = other_ref[:, k * CH : (k + 1) * CH]
        low, high = jnp.where(first, mine, other), jnp.where(first, other, mine)
        kernel = dot(eye, jnp.concatenate([low, high], axis=0), ((1,), (1,)))
        out_ref, at = (one_ref, k) if k < 9 else (two_ref, k - 9)
        out_ref[at * CH : (at + 1) * CH, :] = kernel


VM = pl.BlockSpec(memory_space=pltpu.VMEM)
SM = pl.BlockSpec(memory_space=pltpu.SMEM)
HB = pl.BlockSpec(memory_space=pltpu.HBM)


def call(body, outs, scratch, *args, flops=10**7, scalars=True, far_args=(), far_outs=()):
    moved = sum(math.prod(a.shape) * a.dtype.itemsize for a in args)
    moved += sum(math.prod(s) * jnp.dtype(t).itemsize for s, t in outs)
    args = [pltpu.with_memory_space_constraint(a, pltpu.HBM) if k in far_args else a for k, a in enumerate(args)]
    return pl.pallas_call(
        body,
        cost_estimate=pl.CostEstimate(flops=flops, bytes_accessed=moved, transcendentals=0),
        out_shape=[pltpu.HBM(s, t) if k in far_outs else jax.ShapeDtypeStruct(s, t) for k, (s, t) in enumerate(outs)],
        in_specs=[SM if scalars and k == 0 else HB if k in far_args else VM for k in range(len(args))],
        out_specs=[HB if k in far_outs else VM for k in range(len(outs))],
        scratch_shapes=scratch,
        compiler_params=pltpu.CompilerParams(vmem_limit_bytes=24 << 20),
    )(*args)


def block(
    field, weight_one, bias_one, weight_two, bias_two, depth_levels, fold_partner, cotangent
):
    n_low = lax.axis_size("z")
    n_high = lax.axis_size("yl") * lax.axis_size("x")
    n_z, n_m = n_low * n_high, 4
    swap = [(0, 1), (1, 0)]
    merid = lax.axis_index(MERID)
    core = lax.axis_index("c")
    flat_field = field.reshape(ROWS * COLS, CH)
    flat_cot = cotangent.reshape(ROWS * COLS, CH)
    edge, rim = ((2 * ROWS, LANES), BF16), ((2 * COLS, LANES), BF16)
    flat_deep, top_rows, low_rows, west_edge, east_edge = call(
        pack_kernel,
        [((ROWS * COLS, 128), BF16), rim, rim, edge, ((2 * ROWS + 8, LANES), BF16)],
        [
            pltpu.VMEM((2 * ROWS + 8, LANES), F32),
            pltpu.VMEM((ROWS * COLS, CH), BF16),
            pltpu.VMEM((ROWS * COLS, CH), BF16),
            pltpu.VMEM((ROWS, COLS), jnp.int32),
            pltpu.SemaphoreType.DMA((3,)),
        ],
        flat_field, flat_cot, depth_levels, scalars=False, far_args=(0, 1, 2),
    )

    fold_partner, west_edge = lax.optimization_barrier((fold_partner, west_edge))
    shift = fold_partner[0] + 2
    quotient, rest = shift // COLS % n_z, shift % COLS - 1
    scal = jnp.stack([(merid == n_m - 1).astype(jnp.int32), rest.astype(jnp.int32), core.astype(jnp.int32)])

    def hop(rows, target):
        route = [(m * n_m + n_m - 1, (target(m) % n_z) * n_m + n_m - 1) for m in range(n_z)]
        return lax.ppermute(rows, ZONAL + MERID, route)

    near = hop(top_rows, lambda m: m - 1)
    west = lax.ppermute(east_edge, ZONAL, [(i, (i + 1) % n_z) for i in range(n_z)])
    east = lax.ppermute(west_edge, ZONAL, [((i + 1) % n_z, i) for i in range(n_z)])
    strip = ((2 * PITCH, LANES), BF16)
    inner, outer, fold = call(
        strip_kernel,
        [strip, strip, ((2 * PITCH, 2 * CH), BF16)],
        [
            pltpu.VMEM((2 * ROWS + 8, LANES), F32),
            pltpu.VMEM((2 * ROWS, LANES), F32),
            pltpu.VMEM((16, LANES), F32),
            pltpu.VMEM((2 * PITCH, LANES), F32),
            pltpu.VMEM((2 * PITCH, LANES), F32),
        ],
        scal, top_rows, low_rows, west, east, near,
    )

    def turn(rows, high):
        return hop(rows, lambda m: n_low * ((n_high - 1 - m // n_low + high) % n_high) + m % n_low)

    def slide(rows, low):
        return hop(rows, lambda m: n_low * (m // n_low) + n_low - 1 + low - m % n_low)

    fold = lax.switch(quotient // n_low, [lambda rows, h=h: turn(rows, h) for h in range(n_high)], fold)
    inner, outer, fold = lax.optimization_barrier((inner, outer, fold))
    inner = lax.ppermute(inner, "c", swap)
    outer = lax.ppermute(outer, MERID, [(1, 2), (2, 1)])
    fold = lax.switch(quotient % n_low, [lambda rows, h=h: slide(rows, h) for h in range(n_low)], fold)
    w1 = weight_one.reshape(9, CH, CH)
    w2 = weight_two.reshape(9, CH, CH)
    half = ((CH // 2, 9 * CH), F32)
    pf, pd, ph, slope, keep_two, send_two = call(
        first_kernel,
        [((EXT, 3 * CH), BF16), ((EXT, 3 * CH), BF16), ((MID, 3 * CH), BF16), ((MID, CH), F32), half, half],
        [
            pltpu.VMEM((EXT + 16, CH), F32),
            pltpu.VMEM((EXT, 128), F32),
            pltpu.VMEM((32, LANES), F32),
            pltpu.VMEM((32, LANES), F32),
            pltpu.VMEM((2 * PITCH, LANES), F32),
            pltpu.VMEM((2 * PITCH, LANES), F32),
            pltpu.VMEM((CH, INNER), BF16),
            pltpu.VMEM((9, CH, CH), BF16),
            pltpu.VMEM((MID, 3 * CH), BF16),
            pltpu.SemaphoreType.DMA((2,)),
        ],
        scal, flat_field, flat_cot, flat_deep, west, east, inner, outer, fold, w1, bias_one.reshape(1, CH),
        flops=3 * 10**9, far_args=(9,), far_outs=(2,),
    )
    came_two = lax.ppermute(send_two, "c", swap)
    pe, keep_one, send_one = call(
        second_kernel,
        [((MID, 3 * CH), BF16), half, half],
        [
            pltpu.VMEM((MID + 16, CH), F32),
            pltpu.VMEM((CH, INNER), BF16),
            pltpu.VMEM((MID, 3 * CH), BF16),
            pltpu.SemaphoreType.DMA,
        ],
        scal, pd, pf, slope, w2,
        flops=3 * 10**9, far_outs=(0,),
    )
    came_one = lax.ppermute(send_one, "c", swap)
    output, input_grad = call(
        third_kernel,
        [((ROWS * COLS, CH), BF16), ((ROWS * COLS, CH), BF16)],
        [],
        scal, ph, pe, flat_field, flat_cot, flat_deep, w1, w2, bias_two.reshape(1, CH),
        flops=3 * 10**9,
    )

    n_p = lax.axis_size("yl") * lax.axis_size("x") * lax.axis_size("yh")
    rows = CH // 2 // n_p
    width = 18 * CH
    (sums,) = call(join_kernel, [((CH // 2, width), BF16)], [], keep_one, came_one, keep_two, came_two, scalars=False)
    sums = lax.all_to_all(sums.reshape(n_p, rows, width), PLANE, 0, 0)
    (sums,) = call(total_kernel, [((rows, width), F32)], [], sums, scalars=False)
    part = rows // n_low
    sums = lax.all_to_all(sums.reshape(n_low, part * 36, 128), "z", 0, 0)
    piece = jnp.sum(sums, axis=0).astype(BF16)
    line = lax.all_to_all(jnp.broadcast_to(piece[None], (n_low, part * 36, 128)), "z", 0, 0)
    line = line.reshape(rows, width)
    mine = lax.all_to_all(jnp.broadcast_to(line[None], (n_p, rows, width)), PLANE, 0, 0)
    mine = mine.reshape(CH // 2, width)
    other = lax.ppermute(mine, "c", swap)
    grad_one, grad_two = call(
        last_kernel,
        [((9 * CH, CH), F32), ((9 * CH, CH), F32)],
        [],
        scal, mine, other,
    )
    return (
        output.reshape(ROWS, COLS, CH),
        input_grad.reshape(ROWS, COLS, CH),
        grad_one.reshape(3, 3, CH, CH),
        grad_two.reshape(3, 3, CH, CH),
    )


def solution(mesh):
    fine = Mesh(mesh.devices.reshape(SPLIT + (2, 2)), ZONAL + MERID)
    cells = P(MERID, ZONAL, None)
    return jax.shard_map(
        block,
        mesh=fine,
        in_specs=(cells, P(), P(), P(), P(), P(MERID, ZONAL), P(), cells),
        out_specs=(cells, cells, P(), P()),
        check_vma=False,
    )
```

```python
import math

import jax
import jax.numpy as jnp
from jax import lax
from jax.experimental import pallas as pl
from jax.experimental.pallas import tpu as pltpu
from jax.sharding import Mesh
from jax.sharding import PartitionSpec as P


LEV = 64
SPLIT = (2, 4, 8)
ZONAL = ("yl", "x", "z")
MERID = ("yh", "c")
PLANE = ("yl", "x", "yh")
SCALE = 1.0 / 512.0
ROWS = 16
COLS = 64
CH = 256
PITCH = 72
EXT = 20 * PITCH + 16
MID = 18 * PITCH + 8
INNER = 16 * PITCH
LANES = 2 * CH + 128
HEAD = 8
F32 = jnp.float32
BF16 = jnp.bfloat16
C0 = math.sqrt(2.0 / math.pi)
C1 = 0.044715


def dot(a, b, dims=((1,), (0,))):
    return lax.dot_general(a, b, (dims, ((), ())), preferred_element_type=F32)


def taps(lhs_ref, row, count, w_ref, picks, transposed):
    total = None
    for a, indices in picks:
        lhs = lhs_ref[row + a * PITCH : row + a * PITCH + count, :]
        side = jnp.concatenate([w_ref[k] for k in indices], axis=1 if transposed else 0)
        part = dot(lhs, side, ((1,), (1 if transposed else 0,)))
        total = part if total is None else total + part
    return total


def plain(rows_of=(0, 1, 2)):
    return [(a, [3 * a + b for b in range(3)]) for a in rows_of]


def turned(rows_of=(0, 1, 2)):
    return [(a, [8 - 3 * a - b for b in range(3)]) for a in rows_of]


def shifted(out_ref, src_ref, count):
    step = 112
    for start in range(0, count, step):
        size = min(step, count - start)
        for b in range(3):
            at = HEAD + start + b - 1
            out_ref[start : start + size, b * CH : (b + 1) * CH] = src_ref[at : at + size, :].astype(BF16)


def own_cells(count, first):
    place = (lax.broadcasted_iota(jnp.int32, (count, CH), 0) + first) % PITCH
    return place >= 8


def transposed_own(ref, first, out_ref):
    eye = (
        lax.broadcasted_iota(jnp.int32, (CH, CH), 0) == lax.broadcasted_iota(jnp.int32, (CH, CH), 1)
    ).astype(BF16)
    step = 128
    for start in range(0, INNER, step):
        cells = ref[first + start : first + start + step, CH : 2 * CH].astype(F32)
        cells = jnp.where(own_cells(step, start), cells, 0.0).astype(BF16)
        out_ref[:, start : start + step] = dot(eye, cells, ((1,), (1,))).astype(BF16)


def weight_grad(keep_ref, send_ref, core, turned_ref, patches_ref, row):
    for a in range(3):
        for b in range(3):
            cells = patches_ref[row + a * PITCH : row + a * PITCH + INNER, b * CH : (b + 1) * CH]
            at = (3 * a + b) * CH
            sums = dot(turned_ref[...], cells)
            low, high = sums[: CH // 2], sums[CH // 2 :]
            keep_ref[:, at : at + CH] = jnp.where(core == 0, low, high)
            send_ref[:, at : at + CH] = jnp.where(core == 0, high, low)


def pack_kernel(
    field_far, cot_far, dep_far, deep_ref, top_ref, low_ref, west_ref, east_ref,
    edge, field_ref, cot_ref, dep_ref, sems,
):
    copies = [
        pltpu.make_async_copy(dep_far, dep_ref, sems.at[0]),
        pltpu.make_async_copy(field_far, field_ref, sems.at[1]),
        pltpu.make_async_copy(cot_far, cot_ref, sems.at[2]),
    ]
    for copy in copies:
        copy.start()
    copies[0].wait()
    eye = (
        lax.broadcasted_iota(jnp.int32, (COLS, COLS), 0) == lax.broadcasted_iota(jnp.int32, (COLS, COLS), 1)
    ).astype(F32)
    ones = jnp.ones((COLS, 128), BF16)
    level = (lax.broadcasted_iota(jnp.int32, (1, CH), 1) % LEV).astype(F32)

    def masked(at, count):
        deep = deep_ref[at : at + count, :].astype(F32)
        keep = level < jnp.concatenate([deep, deep], axis=1)
        return jnp.where(keep, cot_ref[at : at + count, :].astype(F32), 0.0)

    for y in range(ROWS):
        line = dep_ref[y : y + 1, :].astype(F32)
        deep_ref[y * COLS : (y + 1) * COLS, :] = dot((eye * line).astype(BF16), ones).astype(BF16)
    copies[1].wait()
    copies[2].wait()
    for out_ref, first in ((top_ref, ROWS - 2), (low_ref, 0)):
        at = first * COLS
        out_ref[:, 0:CH] = field_ref[at : at + 2 * COLS, :]
        out_ref[:, CH : 2 * CH] = masked(at, 2 * COLS).astype(BF16)
        out_ref[:, 2 * CH : LANES] = deep_ref[at : at + 2 * COLS, :]
    for out_ref, column, skip in ((west_ref, 0, 0), (east_ref, COLS - 16, 14)):
        for y in range(ROWS):
            at = y * COLS + column
            cells = slice(2 * y, 2 * y + 2)
            edge[cells, 0:CH] = field_ref[at : at + 16, :].astype(F32)[skip : skip + 2]
            edge[cells, CH : 2 * CH] = masked(at, 16)[skip : skip + 2]
            edge[cells, 2 * CH : LANES] = deep_ref[at : at + 16, :].astype(F32)[skip : skip + 2]
        if skip:
            edge[2 * ROWS : 2 * ROWS + 8, :] = jnp.zeros((8, LANES), F32)
            for k in range(2):
                at = (ROWS - 2 + k) * COLS + column
                cells = slice(2 * ROWS + k, 2 * ROWS + k + 1)
                edge[cells, 0:CH] = field_ref[at : at + 16, :].astype(F32)[skip - 1 : skip]
                edge[cells, CH : 2 * CH] = masked(at, 16)[skip - 1 : skip]
                edge[cells, 2 * CH : LANES] = deep_ref[at : at + 16, :].astype(F32)[skip - 1 : skip]
        out_ref[...] = edge[0 : out_ref.shape[0], :].astype(BF16)


def strip_kernel(
    scal_ref, top_ref, low_ref, west_ref, east_ref, near_ref, inner_ref, outer_ref, fold_ref, west, east, extra,
    upper, lower,
):
    west[...] = west_ref[...].astype(F32)
    east[...] = east_ref[...].astype(F32)
    for strip, rows_ref, first in ((upper, top_ref, ROWS - 2), (lower, low_ref, 0)):
        strip[...] = jnp.zeros(strip.shape, F32)
        for k in range(2):
            y, at = first + k, k * PITCH
            strip[at : at + COLS, :] = rows_ref[k * COLS : (k + 1) * COLS, :].astype(F32)
            strip[at + 64 : at + 66, :] = east[2 * y : 2 * y + 2, :]
            strip[at + 70 : at + 72, :] = west[2 * y : 2 * y + 2, :]
    first = scal_ref[2] == 0
    inner_ref[...] = jnp.where(first, upper[...], lower[...]).astype(BF16)
    outer_ref[...] = jnp.where(first, lower[...], upper[...]).astype(BF16)
    to = lax.broadcasted_iota(jnp.int32, (PITCH, 144), 0)
    at = lax.broadcasted_iota(jnp.int32, (PITCH, 144), 1)
    want = 63 - jnp.where(to >= 70, to - PITCH, to) + scal_ref[1]
    want = jnp.where((to >= 66) & (to < 70), -98, want)
    have = jnp.where(at < 128, at, jnp.where(at < 130, at - 130, jnp.where(at == 130, -3, -99)))
    pick = (want == have).astype(F32).astype(BF16)
    extra[...] = jnp.zeros(extra.shape, F32)
    here = lax.broadcasted_iota(jnp.int32, (PITCH, 128), 0) == lax.broadcasted_iota(jnp.int32, (PITCH, 128), 1)
    third = lax.broadcasted_iota(jnp.int32, (8, 128), 0) == 2
    for j in range(2):
        i = 1 - j
        y = ROWS - 2 + i
        extra[0:2, :] = west[2 * y : 2 * y + 2, :]
        extra[2:3, :] = west[2 * ROWS + i : 2 * ROWS + i + 1, :]
        rows = slice(i * COLS, (i + 1) * COLS)
        cells = jnp.concatenate([top_ref[rows, :], near_ref[rows, :], extra[...].astype(BF16)], axis=0)
        cells = dot(pick, cells)
        fold_ref[j * PITCH : (j + 1) * PITCH, :] = cells[:, : 2 * CH].astype(BF16)
        line = jnp.sum(jnp.where(here, cells[:, 2 * CH :], 0.0), axis=0, keepdims=True)
        free = slice(j * PITCH + COLS, j * PITCH + COLS + 8)
        tile = jnp.where(third, jnp.broadcast_to(line, (8, 128)), cells[COLS:, :128])
        fold_ref[free, 0:128] = tile.astype(BF16)


def first_kernel(
    scal_ref, field_ref, cot_ref, dep_ref, west_ref, east_ref, inner_ref, outer_ref, fold_ref,
    w_far, bias_ref,
    pf_ref, pd_ref, ph_far, slope_ref, keep_ref, send_ref,
    ext, depth, west, east, south, north, back, w_ref, ph_ref, sems,
):
    weights = pltpu.make_async_copy(w_far, w_ref, sems.at[0])
    weights.start()
    top = scal_ref[0] == 1
    west[...] = west_ref[0 : 2 * ROWS, :].astype(F32)
    east[...] = east_ref[...].astype(F32)
    core_first = scal_ref[2] == 0
    inner, outer = inner_ref[...].astype(F32), outer_ref[...].astype(F32)
    south[...] = jnp.where(core_first, outer, inner)
    north[...] = jnp.where(core_first, inner, outer)
    north[:, 0 : 2 * CH] = north[:, 0 : 2 * CH] + fold_ref[...].astype(F32)
    here = lax.broadcasted_iota(jnp.int32, (PITCH, 128), 0) == lax.broadcasted_iota(jnp.int32, (PITCH, 128), 1)
    for j in range(2):
        tile = fold_ref[j * PITCH + COLS : j * PITCH + COLS + 8, 0:128].astype(F32)
        spread = jnp.where(here, jnp.broadcast_to(tile[2:3, :], (PITCH, 128)), 0.0).astype(BF16)
        rows = slice(j * PITCH, (j + 1) * PITCH)
        north[rows, 2 * CH :] = north[rows, 2 * CH :] + dot(spread, jnp.ones((128, 128), BF16))

    def fill(out_ref, lanes, own, width, head):
        if head:
            out_ref[0:head, :] = jnp.zeros((head, width), F32)
        for g in range(21):
            base = head + g * PITCH
            out_ref[base : base + 8, :] = jnp.zeros((8, width), F32)
            y = g - 3
            if 0 <= y < 16:
                out_ref[base : base + 2, :] = east[2 * y : 2 * y + 2, lanes]
            elif -2 <= y < 0:
                at = (y + 2) * PITCH + 64
                out_ref[base : base + 2, :] = south[at : at + 2, lanes]
            elif y >= 16:
                at = (y - 16) * PITCH + 64
                out_ref[base : base + 2, :] = north[at : at + 2, lanes]
            y = g - 2
            if 0 <= y < 16:
                out_ref[base + 6 : base + 8, :] = west[2 * y : 2 * y + 2, lanes]
            elif -2 <= y < 0:
                at = (y + 2) * PITCH + 70
                out_ref[base + 6 : base + 8, :] = south[at : at + 2, lanes]
            elif 16 <= y < 18:
                at = (y - 16) * PITCH + 70
                out_ref[base + 6 : base + 8, :] = north[at : at + 2, lanes]
        for y in range(-2, 18):
            base = head + (y + 2) * PITCH + 8
            if y < 0:
                out_ref[base : base + 64, :] = south[(y + 2) * PITCH : (y + 2) * PITCH + 64, lanes]
            elif y < 16:
                out_ref[base : base + 64, :] = own(y)
            else:
                out_ref[base : base + 64, :] = north[(y - 16) * PITCH : (y - 16) * PITCH + 64, lanes]
        tail = head + 20 * PITCH + 8
        rest = out_ref.shape[0] - tail
        if rest:
            out_ref[tail:, :] = jnp.zeros((rest, width), F32)

    level = lax.broadcasted_iota(jnp.int32, (1, CH), 1) % LEV
    level = level.astype(F32)

    def wet(values):
        return level < jnp.concatenate([values, values], axis=1)

    def own_field(y):
        return field_ref[y * 64 : (y + 1) * 64, :].astype(F32)

    def own_depth(y):
        return dep_ref[y * 64 : (y + 1) * 64, :].astype(F32)

    def own_delta(y):
        cells = cot_ref[y * 64 : (y + 1) * 64, :].astype(F32)
        return jnp.where(wet(own_depth(y)), cells, 0.0)

    fill(ext, slice(0, CH), own_field, CH, HEAD)
    fill(depth, slice(2 * CH, LANES), own_depth, 128, 0)
    shifted(pf_ref, ext, EXT)
    fill(ext, slice(CH, 2 * CH), own_delta, CH, HEAD)
    shifted(pd_ref, ext, EXT)

    bias = bias_ref[...]
    weights.wait()

    def finish(pre, p):
        count = pre.shape[0]
        x = pre + bias
        square = x * x
        t = jnp.tanh(C0 * (x + C1 * (square * x)))
        keep = wet(depth[p : p + count, :])
        half = 0.5 * (1.0 + t)
        hidden = jnp.where(keep, x * half, 0.0).astype(BF16).astype(F32)
        slope = half + (0.5 * C0) * x * (1.0 - t * t) * (1.0 + (3.0 * C1) * square)
        return hidden, jnp.where(keep, slope, 0.0)

    first = 72
    step = 176
    for start in range(first, first + 1232, step):
        hidden, slope = finish(taps(pf_ref, start - PITCH, step, w_ref, plain(), False), start)
        ext[HEAD + start - first : HEAD + start - first + step, :] = hidden
        slope_ref[start - first : start - first + step, :] = slope
    start = 1296
    picks = [(a, [jnp.where(top, 8 - 3 * a - b, 3 * a + b) for b in range(3)]) for a in range(3)]
    hidden, slope = finish(taps(pf_ref, start - PITCH, 80, w_ref, picks, False), start)
    at = start - first
    beyond = lax.broadcasted_iota(jnp.int32, (8, CH), 0) >= 4
    ext[HEAD + at : HEAD + at + 8, :] = jnp.where(beyond, hidden[:8], ext[HEAD + at : HEAD + at + 8, :])
    slope_ref[at : at + 8, :] = jnp.where(beyond, slope[:8], slope_ref[at : at + 8, :])
    ext[HEAD + at + 8 : HEAD + at + 80, :] = hidden[8:]
    slope_ref[at + 8 : at + 80, :] = slope[8:]
    ext[HEAD + MID : HEAD + MID + 8, :] = jnp.zeros((8, CH), F32)
    shifted(ph_ref, ext, MID)
    leave = pltpu.make_async_copy(ph_ref, ph_far, sems.at[1])
    leave.start()
    transposed_own(pd_ref, 144, back)
    weight_grad(keep_ref, send_ref, scal_ref[2], back, ph_ref, 0)
    leave.wait()


def second_kernel(
    scal_ref, pd_ref, pf_ref, slope_ref, w_ref, pe_far, keep_ref, send_ref, ext, back, pe_ref, sem
):
    top = scal_ref[0] == 1
    first = 72
    ext[0:HEAD, :] = jnp.zeros((HEAD, CH), F32)
    ext[HEAD + MID : HEAD + MID + 8, :] = jnp.zeros((8, CH), F32)

    def put(sums, p):
        at = p - first
        count = sums.shape[0]
        delta = (slope_ref[at : at + count, :] * sums).astype(BF16).astype(F32)
        ext[HEAD + at : HEAD + at + count, :] = delta

    step = 232
    for start in range(first, first + 1160, step):
        put(taps(pd_ref, start - PITCH, step, w_ref, turned(), True), start)
    start = 1232
    sums = taps(pd_ref, start - PITCH, 144, w_ref, turned((0,)), True)
    over = [(2, [jnp.where(top, 6 + b, 2 - b) for b in range(3)])]
    sums = sums + taps(pd_ref, start - PITCH, 144, w_ref, over, True)
    middle = taps(pd_ref, start - PITCH, 72, w_ref, turned((1,)), True)
    beside = [(1, [jnp.where(top, 3 + b, 5 - b) for b in range(3)])]
    upper = taps(pd_ref, 1296 - PITCH, 80, w_ref, beside, True)
    beyond = lax.broadcasted_iota(jnp.int32, (8, CH), 0) >= 4
    put(sums[:64] + middle[:64], 1232)
    put(sums[64:72] + jnp.where(beyond, upper[:8], middle[64:]), 1296)
    put(sums[72:] + upper[8:], 1304)
    start = 1224
    gap = taps(pd_ref, start - PITCH, 16, w_ref, turned((0, 1)), True)
    gap = gap + taps(pd_ref, start - PITCH, 16, w_ref, over, True)
    at = start - first
    delta = (slope_ref[at : at + 8, :] * gap[:8]).astype(BF16).astype(F32)
    ext[HEAD + at : HEAD + at + 8, :] = jnp.where(beyond, delta, ext[HEAD + at : HEAD + at + 8, :])
    shifted(pe_ref, ext, MID)
    leave = pltpu.make_async_copy(pe_ref, pe_far, sem)
    leave.start()
    transposed_own(pe_ref, 72, back)
    weight_grad(keep_ref, send_ref, scal_ref[2], back, pf_ref, 72)
    leave.wait()


def third_kernel(
    scal_ref, ph_ref, pe_ref, field_ref, cot_ref, dep_ref, w1_ref, w2_ref, bias_ref, out_ref, in_ref
):
    top = scal_ref[0] == 1
    level = (lax.broadcasted_iota(jnp.int32, (1, CH), 1) % LEV).astype(F32)
    bias = bias_ref[...]

    def wet(at):
        deep = dep_ref[at, :].astype(F32)
        return level < jnp.concatenate([deep, deep], axis=1)

    for y in range(0, 16, 4):
        p = 144 + y * PITCH
        sums = taps(ph_ref, p - 144, 4 * PITCH, w2_ref, plain(), False)
        for k in range(4):
            at = slice((y + k) * 64, (y + k + 1) * 64)
            cells = field_ref[at, :].astype(F32) + sums[k * PITCH + 8 : (k + 1) * PITCH] + bias
            out_ref[at, :] = jnp.where(wet(at), cells, 0.0).astype(BF16)

    def put(cells, y):
        at = slice(y * 64, (y + 1) * 64)
        total = jnp.where(wet(at), cot_ref[at, :].astype(F32), 0.0) + cells
        in_ref[at, :] = total.astype(BF16)

    for y in range(0, 15, 5):
        p = 144 + y * PITCH
        sums = taps(pe_ref, p - 144, 5 * PITCH, w1_ref, turned(), True)
        for k in range(5):
            put(sums[k * PITCH + 8 : (k + 1) * PITCH], y + k)
    p = 144 + 15 * PITCH + 8
    over = [(2, [jnp.where(top, 6 + b, 2 - b) for b in range(3)])]
    sums = taps(pe_ref, p - 144, 64, w1_ref, turned((0, 1)), True)
    put(sums + taps(pe_ref, p - 144, 64, w1_ref, over, True), 15)


def join_kernel(keep_one, came_one, keep_two, came_two, out_ref):
    width = 9 * CH
    for at in range(0, CH // 2, 16):
        rows = slice(at, at + 16)
        out_ref[rows, 0:width] = (keep_one[rows, :] + came_one[rows, :]).astype(BF16)
        out_ref[rows, width:] = (keep_two[rows, :] + came_two[rows, :]).astype(BF16)


def total_kernel(parts_ref, out_ref):
    count, _, width = parts_ref.shape
    step = 512
    for at in range(0, width, step):
        total = parts_ref[0, :, at : at + step].astype(F32)
        for k in range(1, count):
            total = total + parts_ref[k, :, at : at + step].astype(F32)
        out_ref[:, at : at + step] = total


def last_kernel(scal_ref, mine_ref, other_ref, one_far, two_far, turned_ref, sems):
    first = scal_ref[2] == 0
    down = lax.broadcasted_iota(jnp.int32, (CH, CH), 0)
    across = lax.broadcasted_iota(jnp.int32, (CH, CH), 1)
    eye = jnp.where(down == across, SCALE, 0.0).astype(BF16)
    copies = []
    for k in range(18):
        mine = mine_ref[:, k * CH : (k + 1) * CH]
        other = other_ref[:, k * CH : (k + 1) * CH]
        low, high = jnp.where(first, mine, other), jnp.where(first, other, mine)
        kernel = dot(eye, jnp.concatenate([low, high], axis=0), ((1,), (1,)))
        turned_ref[k * CH : (k + 1) * CH, :] = kernel
        out_ref, at = (one_far, k) if k < 9 else (two_far, k - 9)
        copies.append(
            pltpu.make_async_copy(
                turned_ref.at[k * CH : (k + 1) * CH, :], out_ref.at[at * CH : (at + 1) * CH, :], sems.at[k]
            )
        )
        copies[k].start()
    for copy in copies:
        copy.wait()


def piece_kernel(parts_ref, out_ref):
    total = parts_ref[0]
    for k in range(1, parts_ref.shape[0]):
        total = total + parts_ref[k]
    total = total.astype(BF16)
    for k in range(out_ref.shape[0]):
        out_ref[k] = total


VM = pl.BlockSpec(memory_space=pltpu.VMEM)
SM = pl.BlockSpec(memory_space=pltpu.SMEM)
HB = pl.BlockSpec(memory_space=pltpu.HBM)


def call(body, outs, scratch, *args, flops=10**7, scalars=True, far_args=(), far_outs=()):
    moved = sum(math.prod(a.shape) * a.dtype.itemsize for a in args)
    moved += sum(math.prod(s) * jnp.dtype(t).itemsize for s, t in outs)
    args = [pltpu.with_memory_space_constraint(a, pltpu.HBM) if k in far_args else a for k, a in enumerate(args)]
    return pl.pallas_call(
        body,
        cost_estimate=pl.CostEstimate(flops=flops, bytes_accessed=moved, transcendentals=0),
        out_shape=[pltpu.HBM(s, t) if k in far_outs else jax.ShapeDtypeStruct(s, t) for k, (s, t) in enumerate(outs)],
        in_specs=[SM if scalars and k == 0 else HB if k in far_args else VM for k in range(len(args))],
        out_specs=[HB if k in far_outs else VM for k in range(len(outs))],
        scratch_shapes=scratch,
        compiler_params=pltpu.CompilerParams(vmem_limit_bytes=24 << 20),
    )(*args)


def block(
    field, weight_one, bias_one, weight_two, bias_two, depth_levels, fold_partner, cotangent
):
    n_low = lax.axis_size("z")
    n_high = lax.axis_size("yl") * lax.axis_size("x")
    n_z, n_m = n_low * n_high, 4
    swap = [(0, 1), (1, 0)]
    merid = lax.axis_index(MERID)
    core = lax.axis_index("c")
    flat_field = field.reshape(ROWS * COLS, CH)
    flat_cot = cotangent.reshape(ROWS * COLS, CH)
    edge, rim = ((2 * ROWS, LANES), BF16), ((2 * COLS, LANES), BF16)
    flat_deep, top_rows, low_rows, west_edge, east_edge = call(
        pack_kernel,
        [((ROWS * COLS, 128), BF16), rim, rim, edge, ((2 * ROWS + 8, LANES), BF16)],
        [
            pltpu.VMEM((2 * ROWS + 8, LANES), F32),
            pltpu.VMEM((ROWS * COLS, CH), BF16),
            pltpu.VMEM((ROWS * COLS, CH), BF16),
            pltpu.VMEM((ROWS, COLS), jnp.int32),
            pltpu.SemaphoreType.DMA((3,)),
        ],
        flat_field, flat_cot, depth_levels, scalars=False, far_args=(0, 1, 2),
    )

    fold_partner, west_edge = lax.optimization_barrier((fold_partner, west_edge))
    shift = fold_partner[0] + 2
    quotient, rest = shift // COLS % n_z, shift % COLS - 1
    scal = jnp.stack([(merid == n_m - 1).astype(jnp.int32), rest.astype(jnp.int32), core.astype(jnp.int32)])

    def hop(rows, target):
        route = [(m * n_m + n_m - 1, (target(m) % n_z) * n_m + n_m - 1) for m in range(n_z)]
        return lax.ppermute(rows, ZONAL + MERID, route)

    near = hop(top_rows, lambda m: m - 1)
    west = lax.ppermute(east_edge, ZONAL, [(i, (i + 1) % n_z) for i in range(n_z)])
    east = lax.ppermute(west_edge, ZONAL, [((i + 1) % n_z, i) for i in range(n_z)])
    strip = ((2 * PITCH, LANES), BF16)
    inner, outer, fold = call(
        strip_kernel,
        [strip, strip, ((2 * PITCH, 2 * CH), BF16)],
        [
            pltpu.VMEM((2 * ROWS + 8, LANES), F32),
            pltpu.VMEM((2 * ROWS, LANES), F32),
            pltpu.VMEM((16, LANES), F32),
            pltpu.VMEM((2 * PITCH, LANES), F32),
            pltpu.VMEM((2 * PITCH, LANES), F32),
        ],
        scal, top_rows, low_rows, west, east, near,
    )

    def turn(rows, high):
        return hop(rows, lambda m: n_low * ((n_high - 1 - m // n_low + high) % n_high) + m % n_low)

    def slide(rows, low):
        return hop(rows, lambda m: n_low * (m // n_low) + n_low - 1 + low - m % n_low)

    fold = lax.switch(quotient // n_low, [lambda rows, h=h: turn(rows, h) for h in range(n_high)], fold)
    inner, outer, fold = lax.optimization_barrier((inner, outer, fold))
    inner = lax.ppermute(inner, "c", swap)
    outer = lax.ppermute(outer, MERID, [(1, 2), (2, 1)])
    fold = lax.switch(quotient % n_low, [lambda rows, h=h: slide(rows, h) for h in range(n_low)], fold)
    w1 = weight_one.reshape(9, CH, CH)
    w2 = weight_two.reshape(9, CH, CH)
    half = ((CH // 2, 9 * CH), F32)
    pf, pd, ph, slope, keep_two, send_two = call(
        first_kernel,
        [((EXT, 3 * CH), BF16), ((EXT, 3 * CH), BF16), ((MID, 3 * CH), BF16), ((MID, CH), F32), half, half],
        [
            pltpu.VMEM((EXT + 16, CH), F32),
            pltpu.VMEM((EXT, 128), F32),
            pltpu.VMEM((32, LANES), F32),
            pltpu.VMEM((32, LANES), F32),
            pltpu.VMEM((2 * PITCH, LANES), F32),
            pltpu.VMEM((2 * PITCH, LANES), F32),
            pltpu.VMEM((CH, INNER), BF16),
            pltpu.VMEM((9, CH, CH), BF16),
            pltpu.VMEM((MID, 3 * CH), BF16),
            pltpu.SemaphoreType.DMA((2,)),
        ],
        scal, flat_field, flat_cot, flat_deep, west, east, inner, outer, fold, w1, bias_one.reshape(1, CH),
        flops=3 * 10**9, far_args=(9,), far_outs=(2,),
    )
    came_two = lax.ppermute(send_two, "c", swap)
    pe, keep_one, send_one = call(
        second_kernel,
        [((MID, 3 * CH), BF16), half, half],
        [
            pltpu.VMEM((MID + 16, CH), F32),
            pltpu.VMEM((CH, INNER), BF16),
            pltpu.VMEM((MID, 3 * CH), BF16),
            pltpu.SemaphoreType.DMA,
        ],
        scal, pd, pf, slope, w2,
        flops=3 * 10**9, far_outs=(0,),
    )
    came_one = lax.ppermute(send_one, "c", swap)
    output, input_grad = call(
        third_kernel,
        [((ROWS * COLS, CH), BF16), ((ROWS * COLS, CH), BF16)],
        [],
        scal, ph, pe, flat_field, flat_cot, flat_deep, w1, w2, bias_two.reshape(1, CH),
        flops=3 * 10**9,
    )

    n_p = lax.axis_size("yl") * lax.axis_size("x") * lax.axis_size("yh")
    rows = CH // 2 // n_p
    width = 18 * CH
    (sums,) = call(join_kernel, [((CH // 2, width), BF16)], [], keep_one, came_one, keep_two, came_two, scalars=False)
    sums = lax.all_to_all(sums.reshape(n_p, rows, width), PLANE, 0, 0)
    (sums,) = call(total_kernel, [((rows, width), F32)], [], sums, scalars=False)
    part = rows // n_low
    sums = lax.all_to_all(sums.reshape(n_low, part * 36, 128), "z", 0, 0)
    (piece,) = call(piece_kernel, [((n_low, part * 36, 128), BF16)], [], sums, scalars=False)
    line = lax.all_to_all(piece, "z", 0, 0)
    line = line.reshape(rows, width)
    mine = lax.all_to_all(jnp.broadcast_to(line[None], (n_p, rows, width)), PLANE, 0, 0)
    mine = mine.reshape(CH // 2, width)
    other = lax.ppermute(mine, "c", swap)
    grad_one, grad_two = call(
        last_kernel,
        [((9 * CH, CH), F32), ((9 * CH, CH), F32)],
        [pltpu.VMEM((18 * CH, CH), F32), pltpu.SemaphoreType.DMA((18,))],
        scal, mine, other, far_outs=(0, 1),
    )
    return (
        output.reshape(ROWS, COLS, CH),
        input_grad.reshape(ROWS, COLS, CH),
        grad_one.reshape(3, 3, CH, CH),
        grad_two.reshape(3, 3, CH, CH),
    )


def solution(mesh):
    fine = Mesh(mesh.devices.reshape(SPLIT + (2, 2)), ZONAL + MERID)
    cells = P(MERID, ZONAL, None)
    return jax.shard_map(
        block,
        mesh=fine,
        in_specs=(cells, P(), P(), P(), P(), P(MERID, ZONAL), P(), cells),
        out_specs=(cells, cells, P(), P()),
        check_vma=False,
    )
```
